256 devices in a mesh: layer: 2 (over z_hi), row: 16 (over y, x), col: 8 (over z_lo, core).
Axes of the slice: x: 4, y: 4, z: 8 (z_hi: 2, z_lo: 4; z = z_hi * 4 + z_lo), core: 2. Of those that a mesh axis runs over, the one named last changes fastest.
Arguments:
- root_rhs: float32 [32, 8, 1024], P(None, None, 'row'), may hold values from -6 to 6
- child_rhs: float32 [2, 32, 8, 1024], P('layer', None, None, 'row'), may hold values from -6 to 6
- root_factor: float32 [8, 8, 1024, 1024], P(None, None, 'row', 'col'), may hold values from -0.0625 to 0.0625
- child_factor: float32 [2, 8, 8, 1024, 1024], P('layer', None, None, 'row', 'col'), may hold values from -0.0625 to 0.0625
- coupling: float32 [2, 8, 8, 1024, 1024], P('layer', None, None, 'row', 'col'), may hold values from -0.0234375 to 0.0234375
- root_inverse: float32 [8, 1024, 1024], P(None, 'col', 'row'), as said below
- child_inverse: float32 [2, 8, 1024, 1024], P('layer', None, 'col', 'row'), as said below
Outputs:
- root_solution: float32 [32, 8, 1024], P(None, None, 'row')
- child_solution: float32 [2, 32, 8, 1024], P('layer', None, None, 'row')
The draws below stay inside these ranges and needn't reach their ends.
Inputs may be any that keep to these rules, and one draw needn't show every extreme that they name: Each block of root_inverse is lower triangular. Each block of child_inverse is lower triangular.
All inputs are finite; a program needn't handle non-finite values.
Results may differ from the reference program's by a relative error of at most 0.00015.
Values sent between devices are 32-bit elements; how exact they have to be, the bound alone decides.
A program may use at most 64 MiB of HBM per device.

```python
import jax
import jax.numpy as jnp
from jax import lax

ROOT = 8192
CHILD = 8192
BLK = 1024
NRHS = 32
RB = 8
CB = 8


def lower_inverses(key, amount):
    off_key, diag_key = jax.random.split(key)
    lower_part = jax.random.normal(off_key, (amount, BLK, BLK), jnp.float32) * (0.5 / jnp.sqrt(BLK * 1.0))
    diagonal = jax.random.uniform(diag_key, (amount, BLK), jnp.float32, 0.5, 1.5)
    identity = jnp.eye(BLK, dtype=jnp.float32)
    return jnp.tril(lower_part, -1) + diagonal[:, :, None] * identity[None]


def draw_root_inverse(key, part):
    amount = ROOT // BLK
    return lower_inverses(jax.random.fold_in(key, 11), amount)


def draw_child_inverse(key, part):
    amount = CHILD // BLK
    return lower_inverses(jax.random.fold_in(key, 23), 2 * amount).reshape(2, amount, BLK, BLK)


def level_of(stream_key, shape, cuts, least, largest):
    loudness, own = 1.0, jax.random.fold_in(stream_key, 6)
    for axis_at, blocks in cuts:
        draws = jnp.exp(jax.random.uniform(jax.random.fold_in(own, axis_at), (blocks,), jnp.float32, least / len(cuts), largest / len(cuts)))
        loudness = loudness * jnp.repeat(draws, shape[axis_at] // blocks).reshape([-1 if axis == axis_at else 1 for axis in range(len(shape))])
    return loudness


def bell_draw(key, extent, spread, most, pieces=(), kind=jnp.bfloat16):
    level = level_of(key, extent, pieces, -0.22, 0.18) if pieces else 1.0
    result = jax.random.normal(key, extent, jnp.float32) * spread * level
    return jnp.minimum(jnp.maximum(result, -most), most).astype(kind)


def setup_inputs(seed: int = 0) -> dict:
    splits = jax.random.split(jax.random.key(seed), 8)
    root_rhs = bell_draw(splits[0], (NRHS, RB, BLK), 1.0, 6.0, ((2, 16),), jnp.float32)
    child_rhs = bell_draw(splits[1], (2, NRHS, CB, BLK), 1.0, 6.0, ((0, 2), (3, 16)), jnp.float32)
    root_factor = bell_draw(splits[2], (RB, RB, BLK, BLK), ((ROOT + CHILD) // 2) ** -0.5, 0.0625, ((2, 16), (3, 8)), jnp.float32)
    child_factor = bell_draw(splits[3], (2, CB, CB, BLK, BLK), ((ROOT + CHILD) // 2) ** -0.5, 0.0625, ((0, 2), (3, 16), (4, 8)), jnp.float32)
    coupling = bell_draw(splits[4], (2, RB, CB, BLK, BLK), (4 * (ROOT + CHILD)) ** -0.5, 0.0234375, ((0, 2), (3, 16), (4, 8)), jnp.float32)
    root_inverse = draw_root_inverse(jax.random.fold_in(splits[7], 71), 0)
    child_inverse = draw_child_inverse(jax.random.fold_in(splits[7], 71), 0)
    return {"root_rhs": root_rhs, "child_rhs": child_rhs, "root_factor": root_factor, "child_factor": child_factor, "coupling": coupling, "root_inverse": root_inverse, "child_inverse": child_inverse}


precise = lax.Precision.HIGHEST


def forward(factor, inverse, right, lifted):
    blocks = factor.shape[0]
    solved = jnp.zeros((blocks, right.shape[0], BLK), jnp.float32)
    for target in range(blocks):
        pending = right[:, target] - lifted[target]
        if target > 0:
            pending = pending - jnp.einsum("jnb,jab->na", solved[:target], factor[target, :target], precision=precise)
        solved = solved.at[target].set(jnp.einsum("nb,ab->na", pending, inverse[target], precision=precise))
    return solved


def backward(factor, inverse, values, lifted):
    blocks = factor.shape[0]
    solved = jnp.zeros((blocks, values.shape[1], BLK), jnp.float32)
    for target in reversed(range(blocks)):
        pending = values[target] - lifted[target]
        if target + 1 < blocks:
            pending = pending - jnp.einsum("ina,iab->nb", solved[target + 1:], factor[target + 1:, target], precision=precise)
        solved = solved.at[target].set(jnp.dot(pending, inverse[target], precision=precise))
    return solved


def reference(root_rhs, child_rhs, root_factor, child_factor, coupling, root_inverse, child_inverse):
    root_count = ROOT // BLK
    child_count = CHILD // BLK
    empty_child = jnp.zeros((child_count, NRHS, BLK), jnp.float32)
    child_forward = [forward(child_factor[layer], child_inverse[layer], child_rhs[layer], empty_child) for layer in range(2)]
    lifted = jnp.zeros((root_count, NRHS, BLK), jnp.float32)
    for layer in range(2):
        lifted = lifted + jnp.einsum("jnb,kjab->kna", child_forward[layer], coupling[layer], precision=precise)
    root_forward = forward(root_factor, root_inverse, root_rhs, lifted)
    root_solved = backward(root_factor, root_inverse, root_forward, jnp.zeros((root_count, NRHS, BLK), jnp.float32))
    child_outputs = []
    for layer in range(2):
        lowered = jnp.einsum("ina,ijab->jnb", root_solved, coupling[layer], precision=precise)
        child_solved = backward(child_factor[layer], child_inverse[layer], child_forward[layer], lowered)
        child_outputs.append(jnp.transpose(child_solved, (1, 0, 2)))
    root_solution = jnp.transpose(root_solved, (1, 0, 2))
    return root_solution, jnp.stack(child_outputs, 0)
```

```python
import jax
import jax.numpy as jnp
from jax import lax
from jax.experimental import pallas as pl
from jax.experimental.pallas import tpu as pltpu
from jax.sharding import PartitionSpec as P

MESH = pl.DeviceIdType.MESH
BLOCKS = 8
ROWS = 16
COLS = 8


def dot_t(x, y):
    return lax.dot_general(
        x, y, (((1,), (1,)), ((), ())), precision=lax.Precision.HIGHEST,
        preferred_element_type=jnp.float32,
    )


def dot_n(x, y):
    return lax.dot_general(
        x, y, (((1,), (0,)), ((), ())), precision=lax.Precision.HIGHEST,
        preferred_element_type=jnp.float32,
    )


def pack(x):
    half = x.shape[0] // 2
    return jnp.concatenate([x[:half], x[half:]], axis=1)


def unpack(x):
    half = x.shape[1] // 2
    return jnp.concatenate([x[:, :half], x[:, half:]], axis=0)


def kernel(
    root_rhs, child_rhs, root_factor, child_factor, coupling, root_inv, child_inv,
    root_out, child_out,
    u_ref, v_ref, s_half, acc, col_buf, row_buf, lift_buf, lift_in, s_in,
    col_send, col_recv, row_send, row_recv, pair_send, pair_recv, s_send, s_recv,
):
    layer = lax.axis_index("layer")
    row = lax.axis_index("row")
    col = lax.axis_index("col")
    other = (1 - layer, row, col)
    col_peers = [lax.rem(col + k, COLS) for k in range(1, COLS)]
    row_peers = [lax.rem(row + k, ROWS) for k in range(1, ROWS)]

    barrier = pltpu.get_barrier_semaphore()
    for peer in col_peers:
        pl.semaphore_signal(barrier, inc=1, device_id=(layer, row, peer), device_id_type=MESH)
    for peer in row_peers:
        pl.semaphore_signal(barrier, inc=1, device_id=(layer, peer, col), device_id_type=MESH)
    pl.semaphore_signal(barrier, inc=1, device_id=other, device_id_type=MESH)
    acc[...] = jnp.zeros_like(acc)
    pl.semaphore_wait(barrier, COLS + ROWS - 1)

    def col_copy(par, slot, at, height, peer):
        return pltpu.make_async_remote_copy(
            src_ref=col_buf.at[par, slot, pl.ds(0, height)],
            dst_ref=col_buf.at[par, slot, pl.ds(0, height)],
            send_sem=col_send.at[par, at],
            recv_sem=col_recv.at[par, slot],
            device_id=(layer, row, peer),
            device_id_type=MESH,
        )

    def row_copy(par, slot, at, height, peer):
        return pltpu.make_async_remote_copy(
            src_ref=row_buf.at[par, slot, pl.ds(0, height)],
            dst_ref=row_buf.at[par, slot, pl.ds(0, height)],
            send_sem=row_send.at[par, at],
            recv_sem=row_recv.at[par, slot],
            device_id=(layer, peer, col),
            device_id_type=MESH,
        )

    def over_col(par, value, beside):
        packed = pack(value)
        height = packed.shape[0]
        col_buf[par, col, 0:height] = packed
        for at, peer in enumerate(col_peers):
            col_copy(par, col, at, height, peer).start()
        beside()
        for at, peer in enumerate(col_peers):
            col_copy(par, peer, at, height, peer).wait_recv()
        total = col_buf[par, 0, 0:height]
        for slot in range(1, COLS):
            total = total + col_buf[par, slot, 0:height]
        for at, peer in enumerate(col_peers):
            col_copy(par, col, at, height, peer).wait_send()
        return unpack(total)

    def over_row(par, value, beside):
        height = value.shape[0]
        row_buf[par, row, 0:height] = value
        for at, peer in enumerate(row_peers):
            row_copy(par, row, at, height, peer).start()
        beside()
        for at, peer in enumerate(row_peers):
            row_copy(par, peer, at, height, peer).wait_recv()
        total = row_buf[par, 0, 0:height]
        for slot in range(1, ROWS):
            total = total + row_buf[par, slot, 0:height]
        for at, peer in enumerate(row_peers):
            row_copy(par, row, at, height, peer).wait_send()
        return total

    nrhs = child_rhs.shape[1]
    half = nrhs // 2
    mine = layer * half
    theirs = (1 - layer) * half

    def child_forward(k, carry):
        par = lax.rem(k, 2)
        before = jnp.maximum(k - 1, 0)

        def trailing():
            value = u_ref[before]

            @pl.loop(k + 1, BLOCKS)
            def _(later):
                @pl.when(k > 0)
                def _():
                    acc[later, :, 0:64] += dot_t(value, child_factor[later, before])

        def lifting():
            @pl.when(k > 0)
            def _():
                value = u_ref[before]

                @pl.loop(0, BLOCKS)
                def _(at):
                    lift_buf[at] += dot_t(value, coupling[at, before])

        pending = child_rhs[k] - over_col(par, acc[k, :, 0:64], trailing)
        value = over_row(par, dot_t(pending, child_inv[k]), lifting)
        u_ref[k] = value
        after = jnp.minimum(k + 1, BLOCKS - 1)

        @pl.when(k < BLOCKS - 1)
        def _():
            acc[after, :, 0:64] += dot_t(value, child_factor[after, k])

        return carry

    lift_buf[...] = jnp.zeros_like(lift_buf)
    lax.fori_loop(0, BLOCKS, child_forward, 0)
    last = u_ref[BLOCKS - 1]
    for at in range(BLOCKS):
        lift_buf[at] += dot_t(last, coupling[at, BLOCKS - 1])
    lift_copy = pltpu.make_async_remote_copy(
        src_ref=lift_buf.at[:, pl.ds(theirs, half)],
        dst_ref=lift_in,
        send_sem=pair_send,
        recv_sem=pair_recv,
        device_id=other,
        device_id_type=MESH,
    )
    lift_copy.start()
    lift_copy.wait_recv()
    for at in range(BLOCKS):
        acc[at, 0:half, 0:64] = lift_buf[at, pl.ds(mine, half)] + lift_in[at]
    lift_copy.wait_send()

    def root_forward(k, carry):
        par = lax.rem(k, 2)
        before = jnp.maximum(k - 1, 0)

        def trailing():
            value = v_ref[before]

            @pl.loop(k + 1, BLOCKS)
            def _(later):
                @pl.when(k > 0)
                def _():
                    acc[later, 0:half, 0:64] += dot_t(value, root_factor[later, before])

        pending = root_rhs[k, pl.ds(mine, half)] - over_col(par, acc[k, 0:half, 0:64], trailing)
        value = over_row(par, dot_t(pending, root_inv[k]), lambda: None)
        v_ref[k] = value
        after = jnp.minimum(k + 1, BLOCKS - 1)

        @pl.when(k < BLOCKS - 1)
        def _():
            acc[after, 0:half, 0:64] += dot_t(value, root_factor[after, k])

        return carry

    lax.fori_loop(0, BLOCKS, root_forward, 0)

    acc[...] = jnp.zeros_like(acc)

    def s_copy(k):
        return pltpu.make_async_remote_copy(
            src_ref=s_half.at[k],
            dst_ref=s_in.at[k],
            send_sem=s_send.at[k],
            recv_sem=s_recv.at[k],
            device_id=other,
            device_id_type=MESH,
        )

    def root_backward(step, carry):
        par = lax.rem(step, 2)
        k = BLOCKS - 1 - step
        after = jnp.minimum(k + 1, BLOCKS - 1)

        def trailing():
            value = s_half[after]

            @pl.loop(0, k)
            def _(earlier):
                @pl.when(step > 0)
                def _():
                    acc[earlier, 0:half] += dot_n(value, root_factor[after, earlier])

        pending = v_ref[k] - over_row(par, acc[k, 0:half], trailing)
        value = over_col(par, dot_n(pending, root_inv[k]), lambda: None)
        s_half[k] = value
        s_copy(k).start()
        before = jnp.maximum(k - 1, 0)

        @pl.when(k > 0)
        def _():
            acc[before, 0:half] += dot_n(value, root_factor[k, before])

        return carry

    lax.fori_loop(0, BLOCKS, root_backward, 0)

    acc[...] = jnp.zeros_like(acc)

    @pl.loop(0, BLOCKS)
    def _(step):
        k = BLOCKS - 1 - step
        s_copy(k).wait_recv()
        root_out[k, pl.ds(mine, half)] = s_half[k]
        root_out[k, pl.ds(theirs, half)] = s_in[k]
        value = root_out[k]

        @pl.loop(0, BLOCKS)
        def _(at):
            acc[at] += dot_n(value, coupling[k, at])

        s_copy(k).wait_send()

    def child_backward(step, carry):
        par = lax.rem(step, 2)
        k = BLOCKS - 1 - step
        after = jnp.minimum(k + 1, BLOCKS - 1)

        def trailing():
            value = child_out[after]

            @pl.loop(0, k)
            def _(earlier):
                @pl.when(step > 0)
                def _():
                    acc[earlier] += dot_n(value, child_factor[after, earlier])

        pending = u_ref[k] - over_row(par, acc[k], trailing)
        value = over_col(par, dot_n(pending, child_inv[k]), lambda: None)
        child_out[k] = value
        before = jnp.maximum(k - 1, 0)

        @pl.when(k > 0)
        def _():
            acc[before] += dot_n(value, child_factor[k, before])

        return carry

    lax.fori_loop(0, BLOCKS, child_backward, 0)


def local(root_rhs, child_rhs, root_factor, child_factor, coupling, root_inverse, child_inverse):
    nrhs = root_rhs.shape[0]
    half = nrhs // 2
    wide, thin = root_factor.shape[3], root_factor.shape[2]
    vmem = pl.BlockSpec(memory_space=pltpu.VMEM)
    f32 = jnp.float32
    dma = pltpu.SemaphoreType.DMA
    root, child = pl.pallas_call(
        kernel,
        out_shape=(
            jax.ShapeDtypeStruct((BLOCKS, nrhs, thin), f32),
            jax.ShapeDtypeStruct((BLOCKS, nrhs, thin), f32),
        ),
        in_specs=[vmem] * 7,
        out_specs=[vmem] * 2,
        scratch_shapes=[
            pltpu.VMEM((BLOCKS, nrhs, wide), f32),
            pltpu.VMEM((BLOCKS, half, wide), f32),
            pltpu.VMEM((BLOCKS, half, thin), f32),
            pltpu.VMEM((BLOCKS, nrhs, wide), f32),
            pltpu.VMEM((2, COLS, half, wide), f32),
            pltpu.VMEM((2, ROWS, nrhs, wide), f32),
            pltpu.VMEM((BLOCKS, nrhs, thin), f32),
            pltpu.VMEM((BLOCKS, half, thin), f32),
            pltpu.VMEM((BLOCKS, half, thin), f32),
            dma((2, COLS)), dma((2, COLS)), dma((2, ROWS)), dma((2, ROWS)),
            dma, dma, dma((BLOCKS,)), dma((BLOCKS,)),
        ],
        compiler_params=pltpu.CompilerParams(
            collective_id=0, has_side_effects=True, vmem_limit_bytes=48 << 20
        ),
    )(
        jnp.transpose(root_rhs, (1, 0, 2)),
        jnp.transpose(child_rhs[0], (1, 0, 2)),
        root_factor, child_factor[0], coupling[0], root_inverse, child_inverse[0],
    )
    return jnp.transpose(root, (1, 0, 2)), jnp.transpose(child, (1, 0, 2))[None]


def solution(mesh):
    in_specs = (
        P(None, None, "row"),
        P("layer", None, None, "row"),
        P(None, None, "row", "col"),
        P("layer", None, None, "row", "col"),
        P("layer", None, None, "row", "col"),
        P(None, "col", "row"),
        P("layer", None, "col", "row"),
    )
    out_specs = (P(None, None, "row"), P("layer", None, None, "row"))
    return jax.shard_map(local, mesh=mesh, in_specs=in_specs, out_specs=out_specs, check_vma=False)
```

```python
import jax
import jax.numpy as jnp
from jax import lax
from jax.experimental import pallas as pl
from jax.experimental.pallas import tpu as pltpu
from jax.sharding import PartitionSpec as P

MESH = pl.DeviceIdType.MESH
PAIRS = 4
ROWS = 16
COLS = 8
THIN = 64
WIDE = 128
SINGLES = 4


def dot_t(x, y):
    return lax.dot_general(
        x, y, (((1,), (1,)), ((), ())), precision=lax.Precision.HIGHEST,
        preferred_element_type=jnp.float32,
    )


def dot_n(x, y):
    return lax.dot_general(
        x, y, (((1,), (0,)), ((), ())), precision=lax.Precision.HIGHEST,
        preferred_element_type=jnp.float32,
    )


def pack(x):
    half = x.shape[0] // 2
    return jnp.concatenate([x[:half], x[half:]], axis=1)


def unpack(x):
    half = x.shape[1] // 2
    return jnp.concatenate([x[:, :half], x[:, half:]], axis=0)


def pair_rows(ref, pair, block):
    return ref[pl.ds(2 * pair, 2), block].reshape(2 * THIN, WIDE)


def kernel(
    root_rhs, child_rhs, root_factor, child_factor, coupling, root_wt, child_wt,
    root_out, child_out,
    u_ref, v_ref, s_half, s_in, acc_f, acc_r, acc_b, acc_c, superw,
    col_buf, row_buf, lift_buf, lift_in, a0_buf, c_buf, a1_buf, t_buf, x_buf,
    col_send, col_recv, row_send, row_recv, lift_send, lift_recv, s_send, s_recv,
    team_send, team_recv, t_send, t_recv, x_send, x_recv,
):
    layer = lax.axis_index("layer")
    row = lax.axis_index("row")
    col = lax.axis_index("col")
    other = (1 - layer, row, col)
    col_peers = [lax.rem(col + k, COLS) for k in range(1, COLS)]
    row_peers = [lax.rem(row + k, ROWS) for k in range(1, ROWS)]
    row4, rowm = row // 4, lax.rem(row, 4)
    col2, colm = col // 2, lax.rem(col, 2)
    nrhs = child_rhs.shape[1]
    half = nrhs // 2
    mine = pl.multiple_of(layer * half, half)
    theirs = pl.multiple_of((1 - layer) * half, half)

    barrier = pltpu.get_barrier_semaphore()
    for peer in col_peers:
        pl.semaphore_signal(barrier, inc=1, device_id=(layer, row, peer), device_id_type=MESH)
    for peer in row_peers:
        pl.semaphore_signal(barrier, inc=1, device_id=(layer, peer, col), device_id_type=MESH)
    pl.semaphore_signal(barrier, inc=1, device_id=other, device_id_type=MESH)
    for ref in (acc_f, acc_b, acc_c, lift_buf):
        ref[...] = jnp.zeros_like(ref)
    pl.semaphore_wait(barrier, COLS + ROWS - 1)

    def col_copy(par, slot, at, height, peer):
        where = col_buf.at[par, slot, pl.ds(0, height)]
        return pltpu.make_async_remote_copy(
            src_ref=where, dst_ref=where,
            send_sem=col_send.at[par, at], recv_sem=col_recv.at[par, slot],
            device_id=(layer, row, peer), device_id_type=MESH,
        )

    def row_copy(par, slot, at, height, width, peer):
        where = row_buf.at[par, slot, pl.ds(0, height), pl.ds(0, width)]
        return pltpu.make_async_remote_copy(
            src_ref=where, dst_ref=where,
            send_sem=row_send.at[par, at], recv_sem=row_recv.at[par, slot],
            device_id=(layer, peer, col), device_id_type=MESH,
        )

    def over_col(par, value, beside):
        height = value.shape[0]
        col_buf[par, col, 0:height] = value
        for at, peer in enumerate(col_peers):
            col_copy(par, col, at, height, peer).start()
        beside()
        for at, peer in enumerate(col_peers):
            col_copy(par, peer, at, height, peer).wait_recv()
        total = col_buf[par, 0, 0:height]
        for slot in range(1, COLS):
            total = total + col_buf[par, slot, 0:height]
        for at, peer in enumerate(col_peers):
            col_copy(par, col, at, height, peer).wait_send()
        return total

    def over_row(par, value, beside):
        height, width = value.shape
        row_buf[par, row, 0:height, 0:width] = value
        for at, peer in enumerate(row_peers):
            row_copy(par, row, at, height, width, peer).start()
        beside()
        for at, peer in enumerate(row_peers):
            row_copy(par, peer, at, height, width, peer).wait_recv()
        total = row_buf[par, 0, 0:height, 0:width]
        for slot in range(1, ROWS):
            total = total + row_buf[par, slot, 0:height, 0:width]
        for at, peer in enumerate(row_peers):
            row_copy(par, row, at, height, width, peer).wait_send()
        return total

    def placed(src, dst, recv, send, to_row, to_col, wanted, finish):
        here = jnp.logical_and(to_row == row, to_col == col)

        @pl.when(jnp.logical_and(wanted, jnp.logical_not(here)))
        def _():
            copy = pltpu.make_async_remote_copy(
                src_ref=src, dst_ref=dst, send_sem=send, recv_sem=recv,
                device_id=(layer, to_row, to_col), device_id_type=MESH,
            )
            copy.wait_send() if finish else copy.start()

        if not finish:
            @pl.when(jnp.logical_and(wanted, here))
            def _():
                pltpu.make_async_copy(src, dst, recv).start()

    def to_team(base, wt, factor, finish=False):
        @pl.loop(0, PAIRS)
        def _(turn):
            pair = lax.rem(turn + col, PAIRS)
            team = base + pair
            for j in range(4):
                placed(
                    wt.at[2 * pair], a0_buf.at[col, rowm], team_recv.at[0],
                    team_send.at[team, j], 4 * row4 + j, team, col2 >= row4, finish,
                )
            for i in range(4):
                placed(
                    factor.at[2 * pair + 1, 2 * pair], c_buf.at[col, rowm], team_recv.at[1],
                    team_send.at[team, 4 + i], 4 * i + row4, team, col2 >= i, finish,
                )
            for i in range(4):
                placed(
                    wt.at[2 * pair + 1], a1_buf.at[row, colm], team_recv.at[2],
                    team_send.at[team, 8 + i], 4 * i + col2, team, row4 <= col2, finish,
                )

    def arrived(ref, sem):
        pltpu.make_async_copy(ref, ref, sem).wait()

    def t_copy(slot, at, to):
        return pltpu.make_async_remote_copy(
            src_ref=t_buf.at[slot], dst_ref=t_buf.at[slot],
            send_sem=t_send.at[at], recv_sem=t_recv.at[slot],
            device_id=(layer, 4 * row4 + to, col), device_id_type=MESH,
        )

    def team_first():
        for part in range(4):
            @pl.when(row4 == part)
            def _():
                arrived(a0_buf.at[pl.ds(2 * part, COLS - 2 * part)], team_recv.at[0])
                arrived(c_buf.at[pl.ds(2 * part, COLS - 2 * part)], team_recv.at[1])
        t_buf[rowm] = jnp.zeros((4 * THIN, 4 * THIN), jnp.float32)

        @pl.loop(2 * row4, COLS)
        def _(at):
            t_buf[rowm] += dot_t(
                a0_buf[at].reshape(4 * THIN, WIDE), c_buf[at].reshape(4 * THIN, WIDE)
            )

        for to in range(1, 4):
            @pl.when(to > rowm)
            def _():
                t_copy(rowm, to, to).start()

    def team_second(start):
        if start:
            for part in range(4):
                @pl.when(rowm == part)
                def _():
                    arrived(a1_buf.at[pl.ds(0, 4 * part + 4)], team_recv.at[2])
            for part in range(3):
                @pl.when(part < rowm)
                def _():
                    t_copy(part, 0, part).wait_recv()
            x_buf[...] = jnp.zeros_like(x_buf)

            @pl.loop(0, rowm + 1)
            def _(part):
                for side in range(2):
                    x_buf[side] -= dot_n(
                        t_buf[part],
                        a1_buf[pl.ds(4 * part, 4), side].reshape(4 * THIN, WIDE),
                    )
        for to in range(1, 4):
            @pl.when(jnp.logical_and(to > rowm, not start))
            def _():
                t_copy(rowm, to, to).wait_send()
        for side in range(2):
            for part in range(4):
                placed(
                    x_buf.at[side, pl.ds(part * THIN, THIN)],
                    superw.at[col, pl.ds(0, THIN), pl.ds(WIDE, WIDE)],
                    x_recv.at[col], x_send.at[side, part],
                    4 * row4 + part, 2 * rowm + side, True, not start,
                )

    def inverse_ready(at):
        arrived(superw.at[at, pl.ds(0, THIN), pl.ds(WIDE, WIDE)], x_recv.at[at])

    def fill_superw():
        for base, wt in ((0, child_wt), (PAIRS, root_wt)):
            for pair in range(PAIRS):
                superw[base + pair, 0:THIN, 0:WIDE] = wt[2 * pair]
                superw[base + pair, THIN:, WIDE:] = wt[2 * pair + 1]
                superw[base + pair, THIN:, 0:WIDE] = jnp.zeros((THIN, WIDE), jnp.float32)

    def child_trailing(value, block, first):
        for later in range(first, PAIRS):
            acc_f[later] += dot_t(value, pair_rows(child_factor, later, block))

    def lifting(value, block):
        for at in range(PAIRS):
            lift_buf[at] += dot_t(value, pair_rows(coupling, at, block))

    value = None
    for block in range(SINGLES):
        par = block % 2
        pair, side = block // 2, block % 2
        low, high = side * THIN, (side + 1) * THIN

        def col_work():
            if block == 0:
                fill_superw()
            if block == 1:
                to_team(0, child_wt, child_factor)
            if block > 0:
                child_trailing(value, block - 1, pair + 1)
            if block == 3:
                team_first()

        def row_work():
            if block == 1:
                to_team(PAIRS, root_wt, root_factor)
            if block > 0:
                lifting(value, block - 1)
            if block == 3:
                team_second(True)

        total = unpack(over_col(par, pack(acc_f[pair, :, low:high]), col_work))
        pending = child_rhs[pair, :, low:high] - total
        value_now = over_row(par, dot_n(pending, child_wt[block]), row_work)
        value = value_now
        u_ref[pair, :, side * WIDE:(side + 1) * WIDE] = value
        if side == 0:
            acc_f[pair, :, THIN:] += dot_t(value, child_factor[block + 1, block])
        else:
            acc_f[pair + 1] += dot_t(value, pair_rows(child_factor, pair + 1, block))

    for pair in range(SINGLES // 2, PAIRS):
        par = pair % 2

        def col_work():
            if pair == SINGLES // 2:
                child_trailing(value, SINGLES - 1, pair + 1)
                lifting(value, SINGLES - 1)
            else:
                for side in range(2):
                    child_trailing(
                        value[:, side * WIDE:(side + 1) * WIDE], 2 * pair - 2 + side, pair + 1
                    )

        def row_work():
            if pair > SINGLES // 2:
                for side in range(2):
                    lifting(value[:, side * WIDE:(side + 1) * WIDE], 2 * pair - 2 + side)

        pending = child_rhs[pair] - over_col(par, acc_f[pair], col_work)
        inverse_ready(pair)
        value_now = over_row(par, dot_n(pending, superw[pair]), row_work)
        value = value_now
        u_ref[pair] = value
        if pair + 1 < PAIRS:
            for side in range(2):
                acc_f[pair + 1] += dot_t(
                    value[:, side * WIDE:(side + 1) * WIDE],
                    pair_rows(child_factor, pair + 1, 2 * pair + side),
                )

    def lift_copy(at):
        return pltpu.make_async_remote_copy(
            src_ref=lift_buf.at[at, pl.ds(theirs, half)], dst_ref=lift_in.at[at],
            send_sem=lift_send.at[at], recv_sem=lift_recv.at[at],
            device_id=other, device_id_type=MESH,
        )

    for at in range(PAIRS):
        for side in range(2):
            lift_buf[at] += dot_t(
                value[:, side * WIDE:(side + 1) * WIDE],
                pair_rows(coupling, at, 2 * PAIRS - 2 + side),
            )
        lift_copy(at).start()

    def lift_ready(at):
        lift_copy(at).wait_recv()
        acc_r[at] = lift_buf[at, pl.ds(mine, half)] + lift_in[at]
        lift_copy(at).wait_send()

    lift_ready(0)

    def root_forward(pair, carry):
        par = lax.rem(pair, 2)

        def col_work():
            @pl.when(pair == 0)
            def _():
                for at in range(1, PAIRS):
                    lift_ready(at)

            @pl.when(pair > 0)
            def _():
                before = v_ref[jnp.maximum(pair - 1, 0)]

                @pl.loop(pair + 1, PAIRS)
                def _(later):
                    for side in range(2):
                        acc_r[later] += dot_t(
                            before[:, side * WIDE:(side + 1) * WIDE],
                            pair_rows(root_factor, later, 2 * pair - 2 + side),
                        )

        pending = root_rhs[pair, pl.ds(mine, half)] - over_col(par, acc_r[pair], col_work)
        inverse_ready(PAIRS + pair)
        value = over_row(par, dot_n(pending, superw[PAIRS + pair]), lambda: None)
        v_ref[pair] = value

        @pl.when(pair + 1 < PAIRS)
        def _():
            for side in range(2):
                acc_r[pair + 1] += dot_t(
                    value[:, side * WIDE:(side + 1) * WIDE],
                    pair_rows(root_factor, pair + 1, 2 * pair + side),
                )

        return carry

    lax.fori_loop(0, PAIRS, root_forward, 0)

    def s_copy(pair):
        return pltpu.make_async_remote_copy(
            src_ref=s_half.at[pair], dst_ref=s_in.at[pair],
            send_sem=s_send.at[pair], recv_sem=s_recv.at[pair],
            device_id=other, device_id_type=MESH,
        )

    def root_solved(pair):
        s_copy(pair).wait_recv()
        root_out[pair, pl.ds(mine, half)] = s_half[pair]
        root_out[pair, pl.ds(theirs, half)] = s_in[pair]
        s_copy(pair).wait_send()

    def lower(value, pair, earlier):
        for side in range(2):
            acc_c[earlier, :, side * WIDE:(side + 1) * WIDE] += dot_n(
                value, pair_rows(coupling, pair, 2 * earlier + side)
            )

    def root_backward(step, carry):
        par = lax.rem(step, 2)
        pair = PAIRS - 1 - step
        after = jnp.minimum(pair + 1, PAIRS - 1)

        def row_work():
            @pl.when(step > 0)
            def _():
                value = s_half[after]

                @pl.loop(0, pair)
                def _(earlier):
                    for side in range(2):
                        acc_b[earlier, :, side * WIDE:(side + 1) * WIDE] += dot_n(
                            value, pair_rows(root_factor, after, 2 * earlier + side)
                        )

        def col_work():
            @pl.when(step > 0)
            def _():
                root_solved(after)
                value = root_out[after]

                @pl.loop(0, PAIRS)
                def _(earlier):
                    lower(value, after, earlier)

        pending = v_ref[pair] - over_row(par, acc_b[pair], row_work)
        value = over_col(par, dot_t(pending, superw[PAIRS + pair]), col_work)
        s_half[pair] = value
        s_copy(pair).start()

        @pl.when(pair > 0)
        def _():
            before = jnp.maximum(pair - 1, 0)
            for side in range(2):
                acc_b[before, :, side * WIDE:(side + 1) * WIDE] += dot_n(
                    value, pair_rows(root_factor, pair, 2 * before + side)
                )

        return carry

    lax.fori_loop(0, PAIRS, root_backward, 0)
    root_solved(0)
    last = root_out[0]
    lower(last, 0, PAIRS - 1)
    for at in range(SINGLES // 2):
        inverse_ready(at)

    def child_backward(step, carry):
        par = lax.rem(step, 2)
        pair = PAIRS - 1 - step
        after = jnp.minimum(pair + 1, PAIRS - 1)

        def row_work():
            @pl.when(step == 0)
            def _():
                for earlier in range(PAIRS - 1):
                    lower(root_out[0], 0, earlier)

            @pl.when(step > 0)
            def _():
                value = child_out[after]

                @pl.loop(0, pair)
                def _(earlier):
                    for side in range(2):
                        acc_c[earlier, :, side * WIDE:(side + 1) * WIDE] += dot_n(
                            value, pair_rows(child_factor, after, 2 * earlier + side)
                        )

        def col_work():
            @pl.when(step == 0)
            def _():
                to_team(0, child_wt, child_factor, True)

            @pl.when(step == 1)
            def _():
                to_team(PAIRS, root_wt, root_factor, True)
                team_second(False)

        pending = u_ref[pair] - over_row(par, acc_c[pair], row_work)
        value = over_col(par, dot_t(pending, superw[pair]), col_work)
        child_out[pair] = value

        @pl.when(pair > 0)
        def _():
            before = jnp.maximum(pair - 1, 0)
            for side in range(2):
                acc_c[before, :, side * WIDE:(side + 1) * WIDE] += dot_n(
                    value, pair_rows(child_factor, pair, 2 * before + side)
                )

        return carry

    lax.fori_loop(0, PAIRS, child_backward, 0)


def paired(x):
    return jnp.transpose(x.reshape(x.shape[0], PAIRS, 2 * THIN), (1, 0, 2))


def unpaired(x):
    return jnp.transpose(x, (1, 0, 2)).reshape(x.shape[1], 2 * PAIRS, THIN)


def local(root_rhs, child_rhs, root_factor, child_factor, coupling, root_inverse, child_inverse):
    nrhs = root_rhs.shape[0]
    half = nrhs // 2
    vmem = pl.BlockSpec(memory_space=pltpu.VMEM)
    f32 = jnp.float32
    dma = pltpu.SemaphoreType.DMA
    root, child = pl.pallas_call(
        kernel,
        out_shape=(
            jax.ShapeDtypeStruct((PAIRS, nrhs, 2 * THIN), f32),
            jax.ShapeDtypeStruct((PAIRS, nrhs, 2 * THIN), f32),
        ),
        in_specs=[vmem] * 7,
        out_specs=[vmem] * 2,
        scratch_shapes=[
            pltpu.VMEM((PAIRS, nrhs, 2 * WIDE), f32),
            pltpu.VMEM((PAIRS, half, 2 * WIDE), f32),
            pltpu.VMEM((PAIRS, half, 2 * THIN), f32),
            pltpu.VMEM((PAIRS, half, 2 * THIN), f32),
            pltpu.VMEM((PAIRS, nrhs, 2 * THIN), f32),
            pltpu.VMEM((PAIRS, half, 2 * THIN), f32),
            pltpu.VMEM((PAIRS, half, 2 * WIDE), f32),
            pltpu.VMEM((PAIRS, nrhs, 2 * WIDE), f32),
            pltpu.VMEM((2 * PAIRS, 2 * THIN, 2 * WIDE), f32),
            pltpu.VMEM((2, COLS, nrhs, 2 * THIN), f32),
            pltpu.VMEM((2, ROWS, nrhs, 2 * WIDE), f32),
            pltpu.VMEM((PAIRS, nrhs, 2 * THIN), f32),
            pltpu.VMEM((PAIRS, half, 2 * THIN), f32),
            pltpu.VMEM((COLS, 4, THIN, WIDE), f32),
            pltpu.VMEM((COLS, 4, THIN, WIDE), f32),
            pltpu.VMEM((ROWS, 2, THIN, WIDE), f32),
            pltpu.VMEM((4, 4 * THIN, 4 * THIN), f32),
            pltpu.VMEM((2, 4 * THIN, WIDE), f32),
            dma((2, COLS)), dma((2, COLS)), dma((2, ROWS)), dma((2, ROWS)),
            dma((PAIRS,)), dma((PAIRS,)), dma((PAIRS,)), dma((PAIRS,)),
            dma((2 * PAIRS, 12)), dma((3,)), dma((4,)), dma((4,)),
            dma((2, 4)), dma((2 * PAIRS,)),
        ],
        compiler_params=pltpu.CompilerParams(
            collective_id=0, has_side_effects=True, vmem_limit_bytes=48 << 20
        ),
    )(
        paired(root_rhs), paired(child_rhs[0]),
        root_factor, child_factor[0], coupling[0],
        jnp.swapaxes(root_inverse, 1, 2), jnp.swapaxes(child_inverse[0], 1, 2),
    )
    return unpaired(root), unpaired(child)[None]


def solution(mesh):
    in_specs = (
        P(None, None, "row"),
        P("layer", None, None, "row"),
        P(None, None, "row", "col"),
        P("layer", None, None, "row", "col"),
        P("layer", None, None, "row", "col"),
        P(None, "col", "row"),
        P("layer", None, "col", "row"),
    )
    out_specs = (P(None, None, "row"), P("layer", None, None, "row"))
    return jax.shard_map(local, mesh=mesh, in_specs=in_specs, out_specs=out_specs, check_vma=False)
```

```python
import jax
import jax.numpy as jnp
from jax import lax
from jax.experimental import pallas as pl
from jax.experimental.pallas import tpu as pltpu
from jax.sharding import PartitionSpec as P

MESH = pl.DeviceIdType.MESH
PAIRS = 4
ROWS = 16
COLS = 8
THIN = 64
WIDE = 128
SINGLES = 4


def dot_t(x, y):
    return lax.dot_general(
        x, y, (((1,), (1,)), ((), ())), precision=lax.Precision.HIGHEST,
        preferred_element_type=jnp.float32,
    )


def dot_n(x, y):
    return lax.dot_general(
        x, y, (((1,), (0,)), ((), ())), precision=lax.Precision.HIGHEST,
        preferred_element_type=jnp.float32,
    )


def pack(x):
    half = x.shape[0] // 2
    return jnp.concatenate([x[:half], x[half:]], axis=1)


def unpack(x):
    half = x.shape[1] // 2
    return jnp.concatenate([x[:, :half], x[:, half:]], axis=0)


def pair_rows(ref, pair, block):
    return ref[pl.ds(2 * pair, 2), block].reshape(2 * THIN, WIDE)


def kernel(
    root_rhs, child_rhs, root_factor_hbm, child_factor_hbm, coupling_hbm, root_wt_hbm, child_wt_hbm,
    root_out, child_out,
    root_factor, child_factor, coupling, root_wt, child_wt,
    u_ref, v_ref, s_half, s_in, acc_f, acc_r, acc_b, acc_c, superw,
    col_buf, row_buf, lift_buf, lift_in, a0_buf, c_buf, a1_buf, t_buf, x_buf,
    col_send, col_recv, row_send, row_recv, lift_send, lift_recv, s_send, s_recv,
    team_send, team_recv, t_send, t_recv, x_send, x_recv, in_sem,
):
    layer = lax.axis_index("layer")
    row = lax.axis_index("row")
    col = lax.axis_index("col")
    other = (1 - layer, row, col)
    col_peers = [lax.rem(col + k, COLS) for k in range(1, COLS)]
    row_peers = [lax.rem(row + k, ROWS) for k in range(1, ROWS)]
    row4, rowm = row // 4, lax.rem(row, 4)
    col2, colm = col // 2, lax.rem(col, 2)
    nrhs = child_rhs.shape[1]
    half = nrhs // 2
    mine = pl.multiple_of(layer * half, half)
    theirs = pl.multiple_of((1 - layer) * half, half)

    loads = [
        pltpu.make_async_copy(src, dst, in_sem.at[at])
        for at, (src, dst) in enumerate((
            (child_wt_hbm, child_wt), (child_factor_hbm, child_factor),
            (coupling_hbm, coupling), (root_wt_hbm, root_wt), (root_factor_hbm, root_factor),
        ))
    ]
    for load in loads:
        load.start()
    barrier = pltpu.get_barrier_semaphore()
    for peer in col_peers:
        pl.semaphore_signal(barrier, inc=1, device_id=(layer, row, peer), device_id_type=MESH)
    for peer in row_peers:
        pl.semaphore_signal(barrier, inc=1, device_id=(layer, peer, col), device_id_type=MESH)
    pl.semaphore_signal(barrier, inc=1, device_id=other, device_id_type=MESH)
    for ref in (acc_f, acc_b, acc_c, lift_buf):
        ref[...] = jnp.zeros_like(ref)
    pl.semaphore_wait(barrier, COLS + ROWS - 1)

    def col_copy(par, slot, at, height, peer):
        where = col_buf.at[par, slot, pl.ds(0, height)]
        return pltpu.make_async_remote_copy(
            src_ref=where, dst_ref=where,
            send_sem=col_send.at[par, at], recv_sem=col_recv.at[par, slot],
            device_id=(layer, row, peer), device_id_type=MESH,
        )

    def row_copy(par, slot, at, height, width, peer):
        where = row_buf.at[par, slot, pl.ds(0, height), pl.ds(0, width)]
        return pltpu.make_async_remote_copy(
            src_ref=where, dst_ref=where,
            send_sem=row_send.at[par, at], recv_sem=row_recv.at[par, slot],
            device_id=(layer, peer, col), device_id_type=MESH,
        )

    def over_col(par, value, beside):
        height = value.shape[0]
        col_buf[par, col, 0:height] = value
        for at, peer in enumerate(col_peers):
            col_copy(par, col, at, height, peer).start()
        beside()
        for at, peer in enumerate(col_peers):
            col_copy(par, peer, at, height, peer).wait_recv()
        total = col_buf[par, 0, 0:height]
        for slot in range(1, COLS):
            total = total + col_buf[par, slot, 0:height]
        for at, peer in enumerate(col_peers):
            col_copy(par, col, at, height, peer).wait_send()
        return total

    def over_row(par, value, beside):
        height, width = value.shape
        row_buf[par, row, 0:height, 0:width] = value
        for at, peer in enumerate(row_peers):
            row_copy(par, row, at, height, width, peer).start()
        beside()
        for at, peer in enumerate(row_peers):
            row_copy(par, peer, at, height, width, peer).wait_recv()
        total = row_buf[par, 0, 0:height, 0:width]
        for slot in range(1, ROWS):
            total = total + row_buf[par, slot, 0:height, 0:width]
        for at, peer in enumerate(row_peers):
            row_copy(par, row, at, height, width, peer).wait_send()
        return total

    phases = (
        (0, 2, child_wt, child_factor, 2),
        (2, 2 * layer, root_wt, root_factor, PAIRS + 2 * layer),
        (1, 0, child_wt, child_factor, 0),
    )

    def placed(src, dst, recv, send, to_layer, to_row, to_col, wanted, finish):
        here = jnp.logical_and(
            to_layer == layer, jnp.logical_and(to_row == row, to_col == col)
        )

        @pl.when(jnp.logical_and(wanted, jnp.logical_not(here)))
        def _():
            copy = pltpu.make_async_remote_copy(
                src_ref=src, dst_ref=dst, send_sem=send, recv_sem=recv,
                device_id=(to_layer, to_row, to_col), device_id_type=MESH,
            )
            copy.wait_send() if finish else copy.start()

        if not finish:
            @pl.when(jnp.logical_and(wanted, here))
            def _():
                pltpu.make_async_copy(src, dst, recv).start()

    def to_team(phase, kind, finish=False):
        base, first, wt, factor, _ = phases[phase]
        for which in range(2):
            pair, team = first + which, base + 4 * which
            for at in range(4):
                send = team_send.at[phase, which, 4 * kind + at]
                if kind == 0:
                    placed(
                        wt.at[2 * pair], a0_buf.at[col, rowm], team_recv.at[0], send,
                        layer, 4 * row4 + at, team, col2 >= row4, finish,
                    )
                elif kind == 1:
                    placed(
                        factor.at[2 * pair + 1, 2 * pair], c_buf.at[col, rowm],
                        team_recv.at[1], send,
                        layer, 4 * at + row4, team, col2 >= at, finish,
                    )
                else:
                    placed(
                        wt.at[2 * pair + 1], a1_buf.at[row, colm], team_recv.at[2], send,
                        layer, 4 * at + col2, team, row4 <= col2, finish,
                    )

    def arrived(ref, sem):
        pltpu.make_async_copy(ref, ref, sem).wait()

    def t_copy(slot, at, to):
        return pltpu.make_async_remote_copy(
            src_ref=t_buf.at[slot], dst_ref=t_buf.at[slot],
            send_sem=t_send.at[at], recv_sem=t_recv.at[slot],
            device_id=(layer, 4 * row4 + to, col), device_id_type=MESH,
        )

    def team_first(phase):
        pl.when(lax.rem(col, 4) == phases[phase][0])(team_product)

    def team_second(phase, start=True):
        pl.when(lax.rem(col, 4) == phases[phase][0])(lambda: team_result(phase, start))

    def team_product():
        for part in range(4):
            @pl.when(row4 == part)
            def _():
                arrived(a0_buf.at[pl.ds(2 * part, COLS - 2 * part)], team_recv.at[0])
                arrived(c_buf.at[pl.ds(2 * part, COLS - 2 * part)], team_recv.at[1])
        t_buf[rowm] = jnp.zeros((4 * THIN, 4 * THIN), jnp.float32)

        @pl.loop(2 * row4, COLS)
        def _(at):
            t_buf[rowm] += dot_t(
                a0_buf[at].reshape(4 * THIN, WIDE), c_buf[at].reshape(4 * THIN, WIDE)
            )

        for to in range(1, 4):
            @pl.when(to > rowm)
            def _():
                t_copy(rowm, to, to).start()

    def team_result(phase, start):
        if start:
            for part in range(4):
                @pl.when(rowm == part)
                def _():
                    arrived(a1_buf.at[pl.ds(0, 4 * part + 4)], team_recv.at[2])
            for part in range(3):
                @pl.when(part < rowm)
                def _():
                    t_copy(part, 0, part).wait_recv()
            x_buf[...] = jnp.zeros_like(x_buf)

            @pl.loop(0, rowm + 1)
            def _(part):
                for side in range(2):
                    x_buf[side] -= dot_n(
                        t_buf[part],
                        a1_buf[pl.ds(4 * part, 4), side].reshape(4 * THIN, WIDE),
                    )
        else:
            for to in range(1, 4):
                @pl.when(to > rowm)
                def _():
                    t_copy(rowm, to, to).wait_send()
        slot = phases[phase][4] + col // 4
        for to in range(2):
            if phase != 1 and to == 1:
                continue
            for side in range(2):
                for part in range(4):
                    placed(
                        x_buf.at[side, pl.ds(part * THIN, THIN)],
                        superw.at[slot, pl.ds(0, THIN), pl.ds(WIDE, WIDE)],
                        x_recv.at[slot], x_send.at[to, side, part],
                        layer if to == 0 else 1 - layer,
                        4 * row4 + part, 2 * rowm + side, True, not start,
                    )

    def inverse_ready(at):
        arrived(superw.at[at, pl.ds(0, THIN), pl.ds(WIDE, WIDE)], x_recv.at[at])

    def fill_superw():
        for base, wt in ((0, child_wt), (PAIRS, root_wt)):
            for pair in range(PAIRS):
                superw[base + pair, 0:THIN, 0:WIDE] = wt[2 * pair]
                superw[base + pair, THIN:, WIDE:] = wt[2 * pair + 1]
                superw[base + pair, THIN:, 0:WIDE] = jnp.zeros((THIN, WIDE), jnp.float32)

    def child_trailing(value, block, first):
        for later in range(first, PAIRS):
            acc_f[later] += dot_t(value, pair_rows(child_factor, later, block))

    def lifting(value, block):
        for at in range(PAIRS):
            lift_buf[at] += dot_t(value, pair_rows(coupling, at, block))

    value = None
    for block in range(SINGLES):
        par = block % 2
        pair, side = block // 2, block % 2
        low, high = side * THIN, (side + 1) * THIN

        def col_work():
            child_trailing(value, block - 1, pair + 1)
            if block == 1:
                to_team(0, 0)
            if block == 2:
                to_team(0, 2)
            if block == 3:
                team_first(0)

        def row_work():
            if block == 0:
                loads[1].wait()
                loads[2].wait()
                loads[3].wait()
                loads[4].wait()
                fill_superw()
            else:
                lifting(value, block - 1)
            if block == 1:
                to_team(0, 1)
            if block == 3:
                team_second(0)
                to_team(1, 0)

        pending = child_rhs[pair, :, low:high]
        if block == 0:
            loads[0].wait()
        else:
            pending = pending - unpack(over_col(par, pack(acc_f[pair, :, low:high]), col_work))
        value_now = over_row(par, dot_n(pending, child_wt[block]), row_work)
        value = value_now
        u_ref[pair, :, side * WIDE:(side + 1) * WIDE] = value
        if side == 0:
            acc_f[pair, :, THIN:] += dot_t(value, child_factor[block + 1, block])
        else:
            acc_f[pair + 1] += dot_t(value, pair_rows(child_factor, pair + 1, block))

    for pair in range(SINGLES // 2, PAIRS):
        par = pair % 2

        def col_work():
            if pair == SINGLES // 2:
                to_team(1, 1)
                child_trailing(value, SINGLES - 1, pair + 1)
                lifting(value, SINGLES - 1)
            else:
                for side in range(2):
                    child_trailing(
                        value[:, side * WIDE:(side + 1) * WIDE], 2 * pair - 2 + side, pair + 1
                    )
                team_first(1)

        def row_work():
            if pair == SINGLES // 2:
                to_team(1, 2)
            else:
                for side in range(2):
                    lifting(value[:, side * WIDE:(side + 1) * WIDE], 2 * pair - 2 + side)
                team_second(1)

        pending = child_rhs[pair] - over_col(par, acc_f[pair], col_work)
        inverse_ready(pair)
        value_now = over_row(par, dot_n(pending, superw[pair]), row_work)
        value = value_now
        u_ref[pair] = value
        if pair + 1 < PAIRS:
            for side in range(2):
                acc_f[pair + 1] += dot_t(
                    value[:, side * WIDE:(side + 1) * WIDE],
                    pair_rows(child_factor, pair + 1, 2 * pair + side),
                )

    def lift_copy(at):
        return pltpu.make_async_remote_copy(
            src_ref=lift_buf.at[at, pl.ds(theirs, half)], dst_ref=lift_in.at[at],
            send_sem=lift_send.at[at], recv_sem=lift_recv.at[at],
            device_id=other, device_id_type=MESH,
        )

    for at in range(PAIRS):
        for side in range(2):
            lift_buf[at] += dot_t(
                value[:, side * WIDE:(side + 1) * WIDE],
                pair_rows(coupling, at, 2 * PAIRS - 2 + side),
            )
        lift_copy(at).start()

    def lift_ready(at):
        lift_copy(at).wait_recv()
        acc_r[at] = lift_buf[at, pl.ds(mine, half)] + lift_in[at]
        lift_copy(at).wait_send()

    lift_ready(0)

    def root_forward(pair, carry):
        par = lax.rem(pair, 2)

        def col_work():
            @pl.when(pair == 0)
            def _():
                for at in range(1, PAIRS):
                    lift_ready(at)

            @pl.when(pair > 0)
            def _():
                before = v_ref[jnp.maximum(pair - 1, 0)]

                @pl.loop(pair + 1, PAIRS)
                def _(later):
                    for side in range(2):
                        acc_r[later] += dot_t(
                            before[:, side * WIDE:(side + 1) * WIDE],
                            pair_rows(root_factor, later, 2 * pair - 2 + side),
                        )

        pending = root_rhs[pair, pl.ds(mine, half)] - over_col(par, acc_r[pair], col_work)
        inverse_ready(PAIRS + pair)

        def row_work():
            for kind in range(3):
                pl.when(pair == kind)(lambda: to_team(2, kind))

        value = over_row(par, dot_n(pending, superw[PAIRS + pair]), row_work)
        v_ref[pair] = value

        @pl.when(pair + 1 < PAIRS)
        def _():
            for side in range(2):
                acc_r[pair + 1] += dot_t(
                    value[:, side * WIDE:(side + 1) * WIDE],
                    pair_rows(root_factor, pair + 1, 2 * pair + side),
                )

        return carry

    lax.fori_loop(0, PAIRS, root_forward, 0)

    def s_copy(pair):
        return pltpu.make_async_remote_copy(
            src_ref=s_half.at[pair], dst_ref=s_in.at[pair],
            send_sem=s_send.at[pair], recv_sem=s_recv.at[pair],
            device_id=other, device_id_type=MESH,
        )

    def root_solved(pair):
        s_copy(pair).wait_recv()
        root_out[pair, pl.ds(mine, half)] = s_half[pair]
        root_out[pair, pl.ds(theirs, half)] = s_in[pair]
        s_copy(pair).wait_send()

    def lower(value, pair, earlier):
        for side in range(2):
            acc_c[earlier, :, side * WIDE:(side + 1) * WIDE] += dot_n(
                value, pair_rows(coupling, pair, 2 * earlier + side)
            )

    def root_backward(step, first):
        par = lax.rem(step, 2)
        pair = PAIRS - 1 - step
        after = jnp.minimum(pair + 1, PAIRS - 1)

        def row_work():
            value = s_half[after]

            @pl.loop(0, pair)
            def _(earlier):
                for side in range(2):
                    acc_b[earlier, :, side * WIDE:(side + 1) * WIDE] += dot_n(
                        value, pair_rows(root_factor, after, 2 * earlier + side)
                    )

        def col_work():
            if first:
                team_first(2)
                return
            root_solved(after)
            value = root_out[after]

            @pl.loop(0, PAIRS)
            def _(earlier):
                lower(value, after, earlier)

            pl.when(step == 1)(lambda: team_second(2))

        pending = v_ref[pair]
        if not first:
            pending = pending - over_row(1 - par, acc_b[pair], row_work)
        value = over_col(par, dot_t(pending, superw[PAIRS + pair]), col_work)
        s_half[pair] = value
        s_copy(pair).start()

        @pl.when(pair > 0)
        def _():
            before = jnp.maximum(pair - 1, 0)
            for side in range(2):
                acc_b[before, :, side * WIDE:(side + 1) * WIDE] += dot_n(
                    value, pair_rows(root_factor, pair, 2 * before + side)
                )

        return 0

    root_backward(jnp.int32(0), True)
    lax.fori_loop(1, PAIRS, lambda step, carry: root_backward(step, False), 0)
    root_solved(0)
    last = root_out[0]
    lower(last, 0, PAIRS - 1)
    for at in range(SINGLES // 2):
        inverse_ready(at)

    def child_backward(step, carry):
        par = lax.rem(step, 2)
        pair = PAIRS - 1 - step
        after = jnp.minimum(pair + 1, PAIRS - 1)

        def row_work():
            @pl.when(step == 0)
            def _():
                for earlier in range(PAIRS - 1):
                    lower(root_out[0], 0, earlier)

            @pl.when(step > 0)
            def _():
                value = child_out[after]

                @pl.loop(0, pair)
                def _(earlier):
                    for side in range(2):
                        acc_c[earlier, :, side * WIDE:(side + 1) * WIDE] += dot_n(
                            value, pair_rows(child_factor, after, 2 * earlier + side)
                        )

        def col_work():
            for phase in range(3):
                @pl.when(step == phase)
                def _():
                    for kind in range(3):
                        to_team(phase, kind, True)
                    team_second(phase, False)

        pending = u_ref[pair] - over_row(1 - par, acc_c[pair], row_work)
        value = over_col(par, dot_t(pending, superw[pair]), col_work)
        child_out[pair] = value

        @pl.when(pair > 0)
        def _():
            before = jnp.maximum(pair - 1, 0)
            for side in range(2):
                acc_c[before, :, side * WIDE:(side + 1) * WIDE] += dot_n(
                    value, pair_rows(child_factor, pair, 2 * before + side)
                )

        return carry

    lax.fori_loop(0, PAIRS, child_backward, 0)


def paired(x):
    return jnp.transpose(x.reshape(x.shape[0], PAIRS, 2 * THIN), (1, 0, 2))


def unpaired(x):
    return jnp.transpose(x, (1, 0, 2)).reshape(x.shape[1], 2 * PAIRS, THIN)


def local(root_rhs, child_rhs, root_factor, child_factor, coupling, root_inverse, child_inverse):
    nrhs = root_rhs.shape[0]
    half = nrhs // 2
    vmem = pl.BlockSpec(memory_space=pltpu.VMEM)
    f32 = jnp.float32
    dma = pltpu.SemaphoreType.DMA
    root, child = pl.pallas_call(
        kernel,
        out_shape=(
            jax.ShapeDtypeStruct((PAIRS, nrhs, 2 * THIN), f32),
            jax.ShapeDtypeStruct((PAIRS, nrhs, 2 * THIN), f32),
        ),
        in_specs=[vmem] * 2 + [pl.BlockSpec(memory_space=pltpu.HBM)] * 5,
        out_specs=[vmem] * 2,
        scratch_shapes=[
            pltpu.VMEM(root_factor.shape, f32),
            pltpu.VMEM(root_factor.shape, f32),
            pltpu.VMEM(root_factor.shape, f32),
            pltpu.VMEM((2 * PAIRS, THIN, WIDE), f32),
            pltpu.VMEM((2 * PAIRS, THIN, WIDE), f32),
            pltpu.VMEM((PAIRS, nrhs, 2 * WIDE), f32),
            pltpu.VMEM((PAIRS, half, 2 * WIDE), f32),
            pltpu.VMEM((PAIRS, half, 2 * THIN), f32),
            pltpu.VMEM((PAIRS, half, 2 * THIN), f32),
            pltpu.VMEM((PAIRS, nrhs, 2 * THIN), f32),
            pltpu.VMEM((PAIRS, half, 2 * THIN), f32),
            pltpu.VMEM((PAIRS, half, 2 * WIDE), f32),
            pltpu.VMEM((PAIRS, nrhs, 2 * WIDE), f32),
            pltpu.VMEM((2 * PAIRS, 2 * THIN, 2 * WIDE), f32),
            pltpu.VMEM((2, COLS, nrhs, 2 * THIN), f32),
            pltpu.VMEM((2, ROWS, nrhs, 2 * WIDE), f32),
            pltpu.VMEM((PAIRS, nrhs, 2 * THIN), f32),
            pltpu.VMEM((PAIRS, half, 2 * THIN), f32),
            pltpu.VMEM((COLS, 4, THIN, WIDE), f32),
            pltpu.VMEM((COLS, 4, THIN, WIDE), f32),
            pltpu.VMEM((ROWS, 2, THIN, WIDE), f32),
            pltpu.VMEM((4, 4 * THIN, 4 * THIN), f32),
            pltpu.VMEM((2, 4 * THIN, WIDE), f32),
            dma((2, COLS)), dma((2, COLS)), dma((2, ROWS)), dma((2, ROWS)),
            dma((PAIRS,)), dma((PAIRS,)), dma((PAIRS,)), dma((PAIRS,)),
            dma((3, 2, 12)), dma((3,)), dma((4,)), dma((4,)),
            dma((2, 2, 4)), dma((2 * PAIRS,)), dma((5,)),
        ],
        compiler_params=pltpu.CompilerParams(
            collective_id=0, has_side_effects=True, vmem_limit_bytes=48 << 20
        ),
    )(
        paired(root_rhs), paired(child_rhs[0]),
        root_factor, child_factor[0], coupling[0],
        jnp.swapaxes(root_inverse, 1, 2), jnp.swapaxes(child_inverse[0], 1, 2),
    )
    return unpaired(root), unpaired(child)[None]


def solution(mesh):
    in_specs = (
        P(None, None, "row"),
        P("layer", None, None, "row"),
        P(None, None, "row", "col"),
        P("layer", None, None, "row", "col"),
        P("layer", None, None, "row", "col"),
        P(None, "col", "row"),
        P("layer", None, "col", "row"),
    )
    out_specs = (P(None, None, "row"), P("layer", None, None, "row"))
    return jax.shard_map(local, mesh=mesh, in_specs=in_specs, out_specs=out_specs, check_vma=False)
```

```python
import jax
import jax.numpy as jnp
from jax import lax
from jax.experimental import pallas as pl
from jax.experimental.pallas import tpu as pltpu
from jax.sharding import PartitionSpec as P

MESH = pl.DeviceIdType.MESH
PAIRS = 4
ROWS = 16
COLS = 8
THIN = 64
WIDE = 128
SINGLES = 4


def dot_t(x, y):
    return lax.dot_general(
        x, y, (((1,), (1,)), ((), ())), precision=lax.Precision.HIGHEST,
        preferred_element_type=jnp.float32,
    )


def dot_n(x, y):
    return lax.dot_general(
        x, y, (((1,), (0,)), ((), ())), precision=lax.Precision.HIGHEST,
        preferred_element_type=jnp.float32,
    )


def pack(x):
    half = x.shape[0] // 2
    return jnp.concatenate([x[:half], x[half:]], axis=1)


def unpack(x):
    half = x.shape[1] // 2
    return jnp.concatenate([x[:, :half], x[:, half:]], axis=0)


def pair_rows(ref, pair, block):
    return ref[pl.ds(2 * pair, 2), block].reshape(2 * THIN, WIDE)


def kernel(
    root_rhs, child_rhs, root_factor_hbm, child_factor_hbm, coupling_hbm, root_wt_hbm, child_wt_hbm,
    root_out, child_out,
    root_factor, child_factor, coupling, root_wt, child_wt,
    u_ref, v_ref, s_half, s_in, acc_f, acc_r, acc_b, acc_c, superw,
    col_buf, row_buf, lift_buf, lift_in, a0_buf, c_buf, a1_buf, t_buf, x_out, x_in, x_buf,
    col_send, col_recv, row_send, row_recv, lift_send, lift_recv, s_send, s_recv,
    z_send, z_recv, xy_send, xy_recv, x_send, x_recv, in_sem,
):
    layer = lax.axis_index("layer")
    row = lax.axis_index("row")
    col = lax.axis_index("col")
    other = (1 - layer, row, col)
    col_peers = [lax.rem(col + k, COLS) for k in range(1, COLS)]
    row_peers = [lax.rem(row + k, ROWS) for k in range(1, ROWS)]
    row4, rowm = row // 4, lax.rem(row, 4)
    col2, colm = col // 2, lax.rem(col, 2)
    nrhs = child_rhs.shape[1]
    half = nrhs // 2
    mine = pl.multiple_of(layer * half, half)
    theirs = pl.multiple_of((1 - layer) * half, half)

    loads = [
        pltpu.make_async_copy(src, dst, in_sem.at[at])
        for at, (src, dst) in enumerate((
            (child_wt_hbm, child_wt), (child_factor_hbm, child_factor),
            (coupling_hbm, coupling), (root_wt_hbm, root_wt), (root_factor_hbm, root_factor),
        ))
    ]
    for load in loads:
        load.start()
    barrier = pltpu.get_barrier_semaphore()
    for peer in col_peers:
        pl.semaphore_signal(barrier, inc=1, device_id=(layer, row, peer), device_id_type=MESH)
    for peer in row_peers:
        pl.semaphore_signal(barrier, inc=1, device_id=(layer, peer, col), device_id_type=MESH)
    pl.semaphore_signal(barrier, inc=1, device_id=other, device_id_type=MESH)
    for ref in (acc_f, acc_b, acc_c, lift_buf):
        ref[...] = jnp.zeros_like(ref)
    pl.semaphore_wait(barrier, COLS + ROWS - 1)

    def col_copy(par, slot, at, height, peer):
        where = col_buf.at[par, slot, pl.ds(0, height)]
        return pltpu.make_async_remote_copy(
            src_ref=where, dst_ref=where,
            send_sem=col_send.at[par, at], recv_sem=col_recv.at[par, slot],
            device_id=(layer, row, peer), device_id_type=MESH,
        )

    def row_copy(par, slot, at, height, width, peer):
        where = row_buf.at[par, slot, pl.ds(0, height), pl.ds(0, width)]
        return pltpu.make_async_remote_copy(
            src_ref=where, dst_ref=where,
            send_sem=row_send.at[par, at], recv_sem=row_recv.at[par, slot],
            device_id=(layer, peer, col), device_id_type=MESH,
        )

    def over_col(par, value, beside):
        height = value.shape[0]
        col_buf[par, col, 0:height] = value
        for at, peer in enumerate(col_peers):
            col_copy(par, col, at, height, peer).start()
        beside()
        for at, peer in enumerate(col_peers):
            col_copy(par, peer, at, height, peer).wait_recv()
        total = col_buf[par, 0, 0:height]
        for slot in range(1, COLS):
            total = total + col_buf[par, slot, 0:height]
        for at, peer in enumerate(col_peers):
            col_copy(par, col, at, height, peer).wait_send()
        return total

    def over_row(par, value, beside):
        height, width = value.shape
        row_buf[par, row, 0:height, 0:width] = value
        for at, peer in enumerate(row_peers):
            row_copy(par, row, at, height, width, peer).start()
        beside()
        for at, peer in enumerate(row_peers):
            row_copy(par, peer, at, height, width, peer).wait_recv()
        total = row_buf[par, 0, 0:height, 0:width]
        for slot in range(1, ROWS):
            total = total + row_buf[par, slot, 0:height, 0:width]
        for at, peer in enumerate(row_peers):
            row_copy(par, row, at, height, width, peer).wait_send()
        return total

    phases = (
        (0, 2, child_wt, child_factor, 2),
        (2, 2 * layer, root_wt, root_factor, PAIRS + 2 * layer),
        (1, 0, child_wt, child_factor, 0),
    )

    def placed(src, dst, recv, send, to_layer, to_row, to_col, wanted, finish):
        here = jnp.logical_and(
            to_layer == layer, jnp.logical_and(to_row == row, to_col == col)
        )

        @pl.when(jnp.logical_and(wanted, jnp.logical_not(here)))
        def _():
            copy = pltpu.make_async_remote_copy(
                src_ref=src, dst_ref=dst, send_sem=send, recv_sem=recv,
                device_id=(to_layer, to_row, to_col), device_id_type=MESH,
            )
            copy.wait_send() if finish else copy.start()

        if not finish:
            @pl.when(jnp.logical_and(wanted, here))
            def _():
                pltpu.make_async_copy(src, dst, recv).start()

    def arrived(ref, sem):
        pltpu.make_async_copy(ref, ref, sem).wait()

    def gather_z(phase, finish=False):
        base, first, wt, factor, _ = phases[phase]
        for which in range(2):
            pair, team = first + which, base + 4 * which
            needed = col2 >= row4
            for kind, (src, dst, wanted) in enumerate((
                (wt.at[2 * pair], a0_buf.at[rowm, col], needed),
                (factor.at[2 * pair + 1, 2 * pair], c_buf.at[row4, col], True),
                (wt.at[2 * pair + 1], a1_buf.at[row4, col], needed),
            )):
                placed(
                    src, dst, z_recv.at[kind], z_send.at[phase, which, kind],
                    layer, row, team, wanted, finish,
                )

    def team_copy(src, dst, send, recv, to_row):
        return pltpu.make_async_remote_copy(
            src_ref=src, dst_ref=dst, send_sem=send, recv_sem=recv,
            device_id=(layer, to_row, col), device_id_type=MESH,
        )

    def tail(ref, slot, part):
        return ref.at[slot, pl.ds(2 * part, COLS - 2 * part)]

    def a0_copy(part, slot, to):
        where = tail(a0_buf, slot, part)
        return team_copy(where, where, xy_send.at[0, to], xy_recv.at[0, slot], 4 * row4 + to)

    def c_copy(part, slot, to):
        where = tail(c_buf, slot, part)
        return team_copy(where, where, xy_send.at[1, to], xy_recv.at[1, slot], 4 * to + rowm)

    def a1_copy(part, slot, to):
        where = tail(a1_buf, slot, part)
        return team_copy(where, where, xy_send.at[2, to], xy_recv.at[2, slot], 4 * to + rowm)

    def part_copy(slot, to):
        return team_copy(
            x_out.at[pl.ds(2 * to, 2)], x_in.at[slot],
            xy_send.at[3, to], xy_recv.at[3, slot], 4 * row4 + to,
        )

    def in_team(phase, work):
        pl.when(lax.rem(col, 4) == phases[phase][0])(work)

    def gather_xy():
        arrived(c_buf.at[row4], z_recv.at[1])
        for to in range(4):
            @pl.when(row4 != to)
            def _():
                c_copy(to, row4, to).start()
        for part in range(4):
            @pl.when(row4 == part)
            def _():
                arrived(tail(a0_buf, rowm, part), z_recv.at[0])
                for to in range(4):
                    @pl.when(rowm != to)
                    def _():
                        a0_copy(part, rowm, to).start()
                arrived(tail(a1_buf, row4, part), z_recv.at[2])
                for to in range(4):
                    if to != part:
                        a1_copy(part, row4, to).start()

    def first_product():
        for part in range(4):
            @pl.when(row4 == part)
            def _():
                for slot in range(4):
                    @pl.when(rowm != slot)
                    def _():
                        a0_copy(part, slot, slot).wait_recv()
                    if slot != part:
                        c_copy(part, slot, slot).wait_recv()
        t_buf[...] = jnp.zeros_like(t_buf)

        @pl.loop(2 * row4, COLS)
        def _(at):
            t_buf[...] += dot_t(
                a0_buf[:, at].reshape(4 * THIN, WIDE), c_buf[:, at].reshape(4 * THIN, WIDE)
            )

    def second_product():
        for slot in range(4):
            @pl.when(row4 != slot)
            def _():
                a1_copy(slot, slot, slot).wait_recv()
        for at in range(COLS):
            deep = at // 2 + 1
            x_out[at] = dot_n(
                t_buf[:, 0:deep * THIN], a1_buf[0:deep, at].reshape(deep * THIN, WIDE)
            )
            if at % 2 == 1:
                @pl.when(rowm != at // 2)
                def _():
                    part_copy(rowm, at // 2).start()

    def spread(phase, finish=False):
        if finish:
            for part in range(4):
                @pl.when(row4 == part)
                def _():
                    for to in range(4):
                        @pl.when(rowm != to)
                        def _():
                            a0_copy(part, rowm, to).wait_send()
                        if to != part:
                            a1_copy(part, row4, to).wait_send()
            for to in range(4):
                @pl.when(row4 != to)
                def _():
                    c_copy(to, row4, to).wait_send()
                @pl.when(rowm != to)
                def _():
                    part_copy(rowm, to).wait_send()
        else:
            x_in[rowm] = x_out[pl.ds(2 * rowm, 2)]
            for slot in range(4):
                @pl.when(rowm != slot)
                def _():
                    part_copy(slot, slot).wait_recv()
            for side in range(2):
                x_buf[side] = -(
                    (x_in[0, side] + x_in[1, side]) + (x_in[2, side] + x_in[3, side])
                )
        slot = phases[phase][4] + col // 4
        for to in range(2):
            if phase != 1 and to == 1:
                continue
            for side in range(2):
                for part in range(4):
                    placed(
                        x_buf.at[side, pl.ds(part * THIN, THIN)],
                        superw.at[slot, pl.ds(0, THIN), pl.ds(WIDE, WIDE)],
                        x_recv.at[slot], x_send.at[to, side, part],
                        layer if to == 0 else 1 - layer,
                        4 * row4 + part, 2 * rowm + side, True, finish,
                    )

    def inverse_ready(at):
        arrived(superw.at[at, pl.ds(0, THIN), pl.ds(WIDE, WIDE)], x_recv.at[at])

    def fill_superw():
        for base, wt in ((0, child_wt), (PAIRS, root_wt)):
            for pair in range(PAIRS):
                superw[base + pair, 0:THIN, 0:WIDE] = wt[2 * pair]
                superw[base + pair, THIN:, WIDE:] = wt[2 * pair + 1]
                superw[base + pair, THIN:, 0:WIDE] = jnp.zeros((THIN, WIDE), jnp.float32)

    def child_trailing(value, block, first):
        for later in range(first, PAIRS):
            acc_f[later] += dot_t(value, pair_rows(child_factor, later, block))

    def lifting(value, block):
        for at in range(PAIRS):
            lift_buf[at] += dot_t(value, pair_rows(coupling, at, block))

    value = None
    for block in range(SINGLES):
        par = block % 2
        pair, side = block // 2, block % 2
        low, high = side * THIN, (side + 1) * THIN

        def col_work():
            if block == 1:
                gather_z(0)
            if block == 2:
                in_team(0, gather_xy)
            if block == 3:
                in_team(0, second_product)
            child_trailing(value, block - 1, pair + 1)

        def row_work():
            if block == 0:
                loads[1].wait()
                loads[2].wait()
                loads[3].wait()
                loads[4].wait()
                fill_superw()
            else:
                lifting(value, block - 1)
            if block == 2:
                in_team(0, first_product)
            if block == 3:
                in_team(0, lambda: spread(0))
                gather_z(1)

        pending = child_rhs[pair, :, low:high]
        if block == 0:
            loads[0].wait()
        else:
            pending = pending - unpack(over_col(par, pack(acc_f[pair, :, low:high]), col_work))
        value_now = over_row(par, dot_n(pending, child_wt[block]), row_work)
        value = value_now
        u_ref[pair, :, side * WIDE:(side + 1) * WIDE] = value
        if side == 0:
            acc_f[pair, :, THIN:] += dot_t(value, child_factor[block + 1, block])
        else:
            acc_f[pair + 1] += dot_t(value, pair_rows(child_factor, pair + 1, block))

    for pair in range(SINGLES // 2, PAIRS):
        par = pair % 2

        def col_work():
            if pair == SINGLES // 2:
                in_team(1, gather_xy)
                child_trailing(value, SINGLES - 1, pair + 1)
                lifting(value, SINGLES - 1)
            else:
                for side in range(2):
                    child_trailing(
                        value[:, side * WIDE:(side + 1) * WIDE], 2 * pair - 2 + side, pair + 1
                    )
                in_team(1, second_product)

        def row_work():
            if pair == SINGLES // 2:
                in_team(1, first_product)
            else:
                for side in range(2):
                    lifting(value[:, side * WIDE:(side + 1) * WIDE], 2 * pair - 2 + side)
                in_team(1, lambda: spread(1))

        pending = child_rhs[pair] - over_col(par, acc_f[pair], col_work)
        inverse_ready(pair)
        value_now = over_row(par, dot_n(pending, superw[pair]), row_work)
        value = value_now
        u_ref[pair] = value
        if pair + 1 < PAIRS:
            for side in range(2):
                acc_f[pair + 1] += dot_t(
                    value[:, side * WIDE:(side + 1) * WIDE],
                    pair_rows(child_factor, pair + 1, 2 * pair + side),
                )

    def lift_copy(at):
        return pltpu.make_async_remote_copy(
            src_ref=lift_buf.at[at, pl.ds(theirs, half)], dst_ref=lift_in.at[at],
            send_sem=lift_send.at[at], recv_sem=lift_recv.at[at],
            device_id=other, device_id_type=MESH,
        )

    for at in range(PAIRS):
        for side in range(2):
            lift_buf[at] += dot_t(
                value[:, side * WIDE:(side + 1) * WIDE],
                pair_rows(coupling, at, 2 * PAIRS - 2 + side),
            )
        lift_copy(at).start()

    def lift_ready(at):
        lift_copy(at).wait_recv()
        acc_r[at] = lift_buf[at, pl.ds(mine, half)] + lift_in[at]
        lift_copy(at).wait_send()

    lift_ready(0)

    def root_forward(pair, carry):
        par = lax.rem(pair, 2)

        def col_work():
            @pl.when(pair == 0)
            def _():
                for at in range(1, PAIRS):
                    lift_ready(at)

            @pl.when(pair > 0)
            def _():
                before = v_ref[jnp.maximum(pair - 1, 0)]

                @pl.loop(pair + 1, PAIRS)
                def _(later):
                    for side in range(2):
                        acc_r[later] += dot_t(
                            before[:, side * WIDE:(side + 1) * WIDE],
                            pair_rows(root_factor, later, 2 * pair - 2 + side),
                        )

        pending = root_rhs[pair, pl.ds(mine, half)] - over_col(par, acc_r[pair], col_work)
        inverse_ready(PAIRS + pair)

        def row_work():
            pl.when(pair == 0)(lambda: gather_z(2))
            pl.when(pair == 1)(lambda: in_team(2, gather_xy))
            pl.when(pair == 2)(lambda: in_team(2, first_product))
            pl.when(pair == 3)(lambda: in_team(2, second_product))

        value = over_row(par, dot_n(pending, superw[PAIRS + pair]), row_work)
        v_ref[pair] = value

        @pl.when(pair + 1 < PAIRS)
        def _():
            for side in range(2):
                acc_r[pair + 1] += dot_t(
                    value[:, side * WIDE:(side + 1) * WIDE],
                    pair_rows(root_factor, pair + 1, 2 * pair + side),
                )

        return carry

    lax.fori_loop(0, PAIRS, root_forward, 0)

    def s_copy(pair):
        return pltpu.make_async_remote_copy(
            src_ref=s_half.at[pair], dst_ref=s_in.at[pair],
            send_sem=s_send.at[pair], recv_sem=s_recv.at[pair],
            device_id=other, device_id_type=MESH,
        )

    def root_solved(pair):
        s_copy(pair).wait_recv()
        root_out[pair, pl.ds(mine, half)] = s_half[pair]
        root_out[pair, pl.ds(theirs, half)] = s_in[pair]
        s_copy(pair).wait_send()

    def lower(value, pair, earlier):
        for side in range(2):
            acc_c[earlier, :, side * WIDE:(side + 1) * WIDE] += dot_n(
                value, pair_rows(coupling, pair, 2 * earlier + side)
            )

    def root_backward(step, first):
        par = lax.rem(step, 2)
        pair = PAIRS - 1 - step
        after = jnp.minimum(pair + 1, PAIRS - 1)

        def row_work():
            value = s_half[after]

            @pl.loop(0, pair)
            def _(earlier):
                for side in range(2):
                    acc_b[earlier, :, side * WIDE:(side + 1) * WIDE] += dot_n(
                        value, pair_rows(root_factor, after, 2 * earlier + side)
                    )

        def col_work():
            if first:
                in_team(2, lambda: spread(2))
                return
            root_solved(after)
            value = root_out[after]

            @pl.loop(0, PAIRS)
            def _(earlier):
                lower(value, after, earlier)

        pending = v_ref[pair]
        if not first:
            pending = pending - over_row(1 - par, acc_b[pair], row_work)
        value = over_col(par, dot_t(pending, superw[PAIRS + pair]), col_work)
        s_half[pair] = value
        s_copy(pair).start()

        @pl.when(pair > 0)
        def _():
            before = jnp.maximum(pair - 1, 0)
            for side in range(2):
                acc_b[before, :, side * WIDE:(side + 1) * WIDE] += dot_n(
                    value, pair_rows(root_factor, pair, 2 * before + side)
                )

        return 0

    root_backward(jnp.int32(0), True)
    lax.fori_loop(1, PAIRS, lambda step, carry: root_backward(step, False), 0)
    root_solved(0)
    last = root_out[0]
    lower(last, 0, PAIRS - 1)
    for at in range(SINGLES // 2):
        inverse_ready(at)

    def child_backward(step, carry):
        par = lax.rem(step, 2)
        pair = PAIRS - 1 - step
        after = jnp.minimum(pair + 1, PAIRS - 1)

        def row_work():
            @pl.when(step == 0)
            def _():
                for earlier in range(PAIRS - 1):
                    lower(root_out[0], 0, earlier)

            @pl.when(step > 0)
            def _():
                value = child_out[after]

                @pl.loop(0, pair)
                def _(earlier):
                    for side in range(2):
                        acc_c[earlier, :, side * WIDE:(side + 1) * WIDE] += dot_n(
                            value, pair_rows(child_factor, after, 2 * earlier + side)
                        )

        def col_work():
            for phase in range(3):
                @pl.when(step == phase)
                def _():
                    gather_z(phase, True)
                    in_team(phase, lambda: spread(phase, True))

        pending = u_ref[pair] - over_row(1 - par, acc_c[pair], row_work)
        value = over_col(par, dot_t(pending, superw[pair]), col_work)
        child_out[pair] = value

        @pl.when(pair > 0)
        def _():
            before = jnp.maximum(pair - 1, 0)
            for side in range(2):
                acc_c[before, :, side * WIDE:(side + 1) * WIDE] += dot_n(
                    value, pair_rows(child_factor, pair, 2 * before + side)
                )

        return carry

    lax.fori_loop(0, PAIRS, child_backward, 0)


def paired(x):
    return jnp.transpose(x.reshape(x.shape[0], PAIRS, 2 * THIN), (1, 0, 2))


def unpaired(x):
    return jnp.transpose(x, (1, 0, 2)).reshape(x.shape[1], 2 * PAIRS, THIN)


def local(root_rhs, child_rhs, root_factor, child_factor, coupling, root_inverse, child_inverse):
    nrhs = root_rhs.shape[0]
    half = nrhs // 2
    vmem = pl.BlockSpec(memory_space=pltpu.VMEM)
    f32 = jnp.float32
    dma = pltpu.SemaphoreType.DMA
    root, child = pl.pallas_call(
        kernel,
        out_shape=(
            jax.ShapeDtypeStruct((PAIRS, nrhs, 2 * THIN), f32),
            jax.ShapeDtypeStruct((PAIRS, nrhs, 2 * THIN), f32),
        ),
        in_specs=[vmem] * 2 + [pl.BlockSpec(memory_space=pltpu.HBM)] * 5,
        out_specs=[vmem] * 2,
        scratch_shapes=[
            pltpu.VMEM(root_factor.shape, f32),
            pltpu.VMEM(root_factor.shape, f32),
            pltpu.VMEM(root_factor.shape, f32),
            pltpu.VMEM((2 * PAIRS, THIN, WIDE), f32),
            pltpu.VMEM((2 * PAIRS, THIN, WIDE), f32),
            pltpu.VMEM((PAIRS, nrhs, 2 * WIDE), f32),
            pltpu.VMEM((PAIRS, half, 2 * WIDE), f32),
            pltpu.VMEM((PAIRS, half, 2 * THIN), f32),
            pltpu.VMEM((PAIRS, half, 2 * THIN), f32),
            pltpu.VMEM((PAIRS, nrhs, 2 * THIN), f32),
            pltpu.VMEM((PAIRS, half, 2 * THIN), f32),
            pltpu.VMEM((PAIRS, half, 2 * WIDE), f32),
            pltpu.VMEM((PAIRS, nrhs, 2 * WIDE), f32),
            pltpu.VMEM((2 * PAIRS, 2 * THIN, 2 * WIDE), f32),
            pltpu.VMEM((2, COLS, nrhs, 2 * THIN), f32),
            pltpu.VMEM((2, ROWS, nrhs, 2 * WIDE), f32),
            pltpu.VMEM((PAIRS, nrhs, 2 * THIN), f32),
            pltpu.VMEM((PAIRS, half, 2 * THIN), f32),
            pltpu.VMEM((4, COLS, THIN, WIDE), f32),
            pltpu.VMEM((4, COLS, THIN, WIDE), f32),
            pltpu.VMEM((4, COLS, THIN, WIDE), f32),
            pltpu.VMEM((4 * THIN, 4 * THIN), f32),
            pltpu.VMEM((COLS, 4 * THIN, WIDE), f32),
            pltpu.VMEM((4, 2, 4 * THIN, WIDE), f32),
            pltpu.VMEM((2, 4 * THIN, WIDE), f32),
            dma((2, COLS)), dma((2, COLS)), dma((2, ROWS)), dma((2, ROWS)),
            dma((PAIRS,)), dma((PAIRS,)), dma((PAIRS,)), dma((PAIRS,)),
            dma((3, 2, 3)), dma((3,)), dma((4, 4)), dma((4, 4)),
            dma((2, 2, 4)), dma((2 * PAIRS,)), dma((5,)),
        ],
        compiler_params=pltpu.CompilerParams(
            collective_id=0, has_side_effects=True, vmem_limit_bytes=48 << 20
        ),
    )(
        paired(root_rhs), paired(child_rhs[0]),
        root_factor, child_factor[0], coupling[0],
        jnp.swapaxes(root_inverse, 1, 2), jnp.swapaxes(child_inverse[0], 1, 2),
    )
    return unpaired(root), unpaired(child)[None]


def solution(mesh):
    in_specs = (
        P(None, None, "row"),
        P("layer", None, None, "row"),
        P(None, None, "row", "col"),
        P("layer", None, None, "row", "col"),
        P("layer", None, None, "row", "col"),
        P(None, "col", "row"),
        P("layer", None, "col", "row"),
    )
    out_specs = (P(None, None, "row"), P("layer", None, None, "row"))
    return jax.shard_map(local, mesh=mesh, in_specs=in_specs, out_specs=out_specs, check_vma=False)
```

```python
import jax
import jax.numpy as jnp
from jax import lax
from jax.experimental import pallas as pl
from jax.experimental.pallas import tpu as pltpu
from jax.sharding import PartitionSpec as P

MESH = pl.DeviceIdType.MESH
PAIRS = 4
ROWS = 16
COLS = 8
THIN = 64
WIDE = 128
SINGLES = 4
HALVES = 2


def dot_t(x, y):
    return lax.dot_general(
        x, y, (((1,), (1,)), ((), ())), precision=lax.Precision.HIGHEST,
        preferred_element_type=jnp.float32,
    )


def dot_n(x, y):
    return lax.dot_general(
        x, y, (((1,), (0,)), ((), ())), precision=lax.Precision.HIGHEST,
        preferred_element_type=jnp.float32,
    )


def pack(x):
    half = x.shape[0] // 2
    return jnp.concatenate([x[:half], x[half:]], axis=1)


def unpack(x):
    half = x.shape[1] // 2
    return jnp.concatenate([x[:, :half], x[:, half:]], axis=0)


def pair_rows(ref, pair, block):
    return ref[pl.ds(2 * pair, 2), block].reshape(2 * THIN, WIDE)


def kernel(
    root_rhs, child_rhs, root_factor_hbm, child_factor_hbm, coupling_hbm, root_wt_hbm, child_wt_hbm,
    root_out, child_out,
    root_factor, child_factor, coupling, root_wt, child_wt,
    u_ref, v_ref, s_half, s_in, acc_f, acc_r, acc_b, acc_c, superw,
    col_buf, row_buf, lift_buf, lift_in, a0_buf, c_buf, a1_buf, t_buf, x_out, x_in, x_buf,
    col_send, col_recv, row_send, row_recv, lift_send, lift_recv, s_send, s_recv,
    z_send, z_recv, xy_send, xy_recv, x_send, x_recv, in_sem,
):
    layer = lax.axis_index("layer")
    row = lax.axis_index("row")
    col = lax.axis_index("col")
    other = (1 - layer, row, col)
    col_peers = [lax.rem(col + k, COLS) for k in range(1, COLS)]
    row_peers = [lax.rem(row + k, ROWS) for k in range(1, ROWS)]
    row4, rowm = row // 4, lax.rem(row, 4)
    col2, colm = col // 2, lax.rem(col, 2)
    nrhs = child_rhs.shape[1]
    half = nrhs // 2
    mine = pl.multiple_of(layer * half, half)
    theirs = pl.multiple_of((1 - layer) * half, half)

    loads = [
        pltpu.make_async_copy(src, dst, in_sem.at[at])
        for at, (src, dst) in enumerate((
            (child_wt_hbm, child_wt), (child_factor_hbm, child_factor),
            (coupling_hbm, coupling), (root_wt_hbm, root_wt), (root_factor_hbm, root_factor),
        ))
    ]
    for load in loads:
        load.start()
    barrier = pltpu.get_barrier_semaphore()
    for peer in col_peers:
        pl.semaphore_signal(barrier, inc=1, device_id=(layer, row, peer), device_id_type=MESH)
    for peer in row_peers:
        pl.semaphore_signal(barrier, inc=1, device_id=(layer, peer, col), device_id_type=MESH)
    pl.semaphore_signal(barrier, inc=1, device_id=other, device_id_type=MESH)
    for ref in (acc_f, acc_b, acc_c, lift_buf):
        ref[...] = jnp.zeros_like(ref)
    pl.semaphore_wait(barrier, COLS + ROWS - 1)

    def col_copy(ch, par, slot, at, height, peer):
        where = col_buf.at[ch, par, slot, pl.ds(0, height)]
        return pltpu.make_async_remote_copy(
            src_ref=where, dst_ref=where,
            send_sem=col_send.at[ch, par, at], recv_sem=col_recv.at[ch, par, slot],
            device_id=(layer, row, peer), device_id_type=MESH,
        )

    def row_copy(ch, par, slot, at, height, width, peer):
        where = row_buf.at[ch, par, slot, pl.ds(0, height), pl.ds(0, width)]
        return pltpu.make_async_remote_copy(
            src_ref=where, dst_ref=where,
            send_sem=row_send.at[ch, par, at], recv_sem=row_recv.at[ch, par, slot],
            device_id=(layer, peer, col), device_id_type=MESH,
        )

    def start_col(ch, par, value):
        height = value.shape[0]
        col_buf[ch, par, col, 0:height] = value
        for at, peer in enumerate(col_peers):
            col_copy(ch, par, col, at, height, peer).start()

    def finish_col(ch, par, height):
        for at, peer in enumerate(col_peers):
            col_copy(ch, par, peer, at, height, peer).wait_recv()
        total = col_buf[ch, par, 0, 0:height]
        for slot in range(1, COLS):
            total = total + col_buf[ch, par, slot, 0:height]
        return total

    def drain_col(par, height):
        for ch in range(HALVES):
            for at, peer in enumerate(col_peers):
                col_copy(ch, par, col, at, height, peer).wait_send()

    def start_row(ch, par, value):
        height, width = value.shape
        row_buf[ch, par, row, 0:height, 0:width] = value
        for at, peer in enumerate(row_peers):
            row_copy(ch, par, row, at, height, width, peer).start()

    def finish_row(ch, par, height, width):
        for at, peer in enumerate(row_peers):
            row_copy(ch, par, peer, at, height, width, peer).wait_recv()
        total = row_buf[ch, par, 0, 0:height, 0:width]
        for slot in range(1, ROWS):
            total = total + row_buf[ch, par, slot, 0:height, 0:width]
        return total

    def drain_row(par, height, width):
        for ch in range(HALVES):
            for at, peer in enumerate(row_peers):
                row_copy(ch, par, row, at, height, width, peer).wait_send()

    phases = (
        (0, 2, child_wt, child_factor, 2),
        (2, 2 * layer, root_wt, root_factor, PAIRS + 2 * layer),
        (1, 0, child_wt, child_factor, 0),
    )

    def placed(src, dst, recv, send, to_layer, to_row, to_col, wanted, finish):
        here = jnp.logical_and(
            to_layer == layer, jnp.logical_and(to_row == row, to_col == col)
        )

        @pl.when(jnp.logical_and(wanted, jnp.logical_not(here)))
        def _():
            copy = pltpu.make_async_remote_copy(
                src_ref=src, dst_ref=dst, send_sem=send, recv_sem=recv,
                device_id=(to_layer, to_row, to_col), device_id_type=MESH,
            )
            copy.wait_send() if finish else copy.start()

        if not finish:
            @pl.when(jnp.logical_and(wanted, here))
            def _():
                pltpu.make_async_copy(src, dst, recv).start()

    def arrived(ref, sem):
        pltpu.make_async_copy(ref, ref, sem).wait()

    def gather_z(phase, finish=False):
        base, first, wt, factor, _ = phases[phase]
        for which in range(2):
            pair, team = first + which, base + 4 * which
            needed = col2 >= row4
            for kind, (src, dst, wanted) in enumerate((
                (wt.at[2 * pair], a0_buf.at[rowm, col], needed),
                (factor.at[2 * pair + 1, 2 * pair], c_buf.at[row4, col], True),
                (wt.at[2 * pair + 1], a1_buf.at[row4, col], needed),
            )):
                placed(
                    src, dst, z_recv.at[kind], z_send.at[phase, which, kind],
                    layer, row, team, wanted, finish,
                )

    def team_copy(src, dst, send, recv, to_row):
        return pltpu.make_async_remote_copy(
            src_ref=src, dst_ref=dst, send_sem=send, recv_sem=recv,
            device_id=(layer, to_row, col), device_id_type=MESH,
        )

    def tail(ref, slot, part):
        return ref.at[slot, pl.ds(2 * part, COLS - 2 * part)]

    def a0_copy(part, slot, to):
        where = tail(a0_buf, slot, part)
        return team_copy(where, where, xy_send.at[0, to], xy_recv.at[0, slot], 4 * row4 + to)

    def c_copy(part, slot, to):
        where = tail(c_buf, slot, part)
        return team_copy(where, where, xy_send.at[1, to], xy_recv.at[1, slot], 4 * to + rowm)

    def a1_copy(part, slot, to):
        where = tail(a1_buf, slot, part)
        return team_copy(where, where, xy_send.at[2, to], xy_recv.at[2, slot], 4 * to + rowm)

    def part_copy(slot, to):
        return team_copy(
            x_out.at[pl.ds(2 * to, 2)], x_in.at[slot],
            xy_send.at[3, to], xy_recv.at[3, slot], 4 * row4 + to,
        )

    def in_team(phase, work):
        pl.when(lax.rem(col, 4) == phases[phase][0])(work)

    def gather_xy():
        arrived(c_buf.at[row4], z_recv.at[1])
        for to in range(4):
            @pl.when(row4 != to)
            def _():
                c_copy(to, row4, to).start()
        for part in range(4):
            @pl.when(row4 == part)
            def _():
                arrived(tail(a0_buf, rowm, part), z_recv.at[0])
                for to in range(4):
                    @pl.when(rowm != to)
                    def _():
                        a0_copy(part, rowm, to).start()
                arrived(tail(a1_buf, row4, part), z_recv.at[2])
                for to in range(4):
                    if to != part:
                        a1_copy(part, row4, to).start()

    def first_product():
        for part in range(4):
            @pl.when(row4 == part)
            def _():
                for slot in range(4):
                    @pl.when(rowm != slot)
                    def _():
                        a0_copy(part, slot, slot).wait_recv()
                    if slot != part:
                        c_copy(part, slot, slot).wait_recv()
        t_buf[...] = jnp.zeros_like(t_buf)

        @pl.loop(2 * row4, COLS)
        def _(at):
            t_buf[...] += dot_t(
                a0_buf[:, at].reshape(4 * THIN, WIDE), c_buf[:, at].reshape(4 * THIN, WIDE)
            )

    def second_product():
        for slot in range(4):
            @pl.when(row4 != slot)
            def _():
                a1_copy(slot, slot, slot).wait_recv()
        for at in range(COLS):
            deep = at // 2 + 1
            x_out[at] = dot_n(
                t_buf[:, 0:deep * THIN], a1_buf[0:deep, at].reshape(deep * THIN, WIDE)
            )
            if at % 2 == 1:
                @pl.when(rowm != at // 2)
                def _():
                    part_copy(rowm, at // 2).start()

    def spread(phase, finish=False):
        if finish:
            for part in range(4):
                @pl.when(row4 == part)
                def _():
                    for to in range(4):
                        @pl.when(rowm != to)
                        def _():
                            a0_copy(part, rowm, to).wait_send()
                        if to != part:
                            a1_copy(part, row4, to).wait_send()
            for to in range(4):
                @pl.when(row4 != to)
                def _():
                    c_copy(to, row4, to).wait_send()
                @pl.when(rowm != to)
                def _():
                    part_copy(rowm, to).wait_send()
        else:
            x_in[rowm] = x_out[pl.ds(2 * rowm, 2)]
            for slot in range(4):
                @pl.when(rowm != slot)
                def _():
                    part_copy(slot, slot).wait_recv()
            for side in range(2):
                x_buf[side] = -(
                    (x_in[0, side] + x_in[1, side]) + (x_in[2, side] + x_in[3, side])
                )
        slot = phases[phase][4] + col // 4
        for to in range(2):
            if phase != 1 and to == 1:
                continue
            for side in range(2):
                for part in range(4):
                    placed(
                        x_buf.at[side, pl.ds(part * THIN, THIN)],
                        superw.at[slot, pl.ds(0, THIN), pl.ds(WIDE, WIDE)],
                        x_recv.at[slot], x_send.at[to, side, part],
                        layer if to == 0 else 1 - layer,
                        4 * row4 + part, 2 * rowm + side, True, finish,
                    )

    def inverse_ready(at):
        arrived(superw.at[at, pl.ds(0, THIN), pl.ds(WIDE, WIDE)], x_recv.at[at])

    def fill_superw():
        for base, wt in ((0, child_wt), (PAIRS, root_wt)):
            for pair in range(PAIRS):
                superw[base + pair, 0:THIN, 0:WIDE] = wt[2 * pair]
                superw[base + pair, THIN:, WIDE:] = wt[2 * pair + 1]
                superw[base + pair, THIN:, 0:WIDE] = jnp.zeros((THIN, WIDE), jnp.float32)

    def child_trailing(value, block, first):
        for later in range(first, PAIRS):
            acc_f[later] += dot_t(value, pair_rows(child_factor, later, block))

    def lifting(value, block):
        for at in range(PAIRS):
            lift_buf[at] += dot_t(value, pair_rows(coupling, at, block))

    fine = half // HALVES
    child_rows = [slice(ch * half, (ch + 1) * half) for ch in range(HALVES)]
    root_rows = [slice(ch * fine, (ch + 1) * fine) for ch in range(HALVES)]

    def child_value(ch, block):
        value = finish_row(ch, block % 2, half, WIDE)
        rows, pair, side = child_rows[ch], block // 2, block % 2
        u_ref[pair, rows, side * WIDE:(side + 1) * WIDE] = value
        if side == 0:
            acc_f[pair, rows, THIN:] += dot_t(value, child_factor[block + 1, block])
        else:
            acc_f[pair + 1, rows] += dot_t(value, pair_rows(child_factor, pair + 1, block))

    def child_block(block):
        return u_ref[block // 2, :, (block % 2) * WIDE:(block % 2 + 1) * WIDE]

    loads[0].wait()
    for ch in range(HALVES):
        start_row(ch, 0, dot_n(child_rhs[0, child_rows[ch], 0:THIN], child_wt[0]))
    for load in loads[1:]:
        load.wait()
    fill_superw()
    for block in range(1, SINGLES):
        par = block % 2
        pair, side = block // 2, block % 2
        low, high = side * THIN, (side + 1) * THIN
        for ch in range(HALVES):
            child_value(ch, block - 1)
            start_col(ch, par, pack(acc_f[pair, child_rows[ch], low:high]))
        if block == 1:
            gather_z(0)
        if block == 2:
            in_team(0, gather_xy)
        if block == 3:
            in_team(0, second_product)
        drain_row(1 - par, half, WIDE)
        child_trailing(child_block(block - 1), block - 1, pair + 1)
        for ch in range(HALVES):
            total = unpack(finish_col(ch, par, half // 2))
            pending = child_rhs[pair, child_rows[ch], low:high] - total
            start_row(ch, par, dot_n(pending, child_wt[block]))
        if block == 2:
            in_team(0, first_product)
        if block == 3:
            in_team(0, lambda: spread(0))
            gather_z(1)
        drain_col(par, half // 2)
        lifting(child_block(block - 1), block - 1)

    def child_pair(ch, pair):
        value = finish_row(ch, pair % 2, half, 2 * WIDE)
        rows = child_rows[ch]
        u_ref[pair, rows] = value
        if pair + 1 < PAIRS:
            for side in range(2):
                acc_f[pair + 1, rows] += dot_t(
                    value[:, side * WIDE:(side + 1) * WIDE],
                    pair_rows(child_factor, pair + 1, 2 * pair + side),
                )

    for pair in range(SINGLES // 2, PAIRS):
        par = pair % 2
        opening = pair == SINGLES // 2
        for ch in range(HALVES):
            if opening:
                child_value(ch, SINGLES - 1)
            else:
                child_pair(ch, pair - 1)
            start_col(ch, par, acc_f[pair, child_rows[ch]])
        if opening:
            in_team(1, gather_xy)
            drain_row(1 - par, half, WIDE)
            child_trailing(child_block(SINGLES - 1), SINGLES - 1, pair + 1)
            lifting(child_block(SINGLES - 1), SINGLES - 1)
        else:
            in_team(1, second_product)
            drain_row(1 - par, half, 2 * WIDE)
            for block in (2 * pair - 2, 2 * pair - 1):
                child_trailing(child_block(block), block, pair + 1)
        inverse_ready(pair)
        for ch in range(HALVES):
            pending = child_rhs[pair, child_rows[ch]] - finish_col(ch, par, half)
            start_row(ch, par, dot_n(pending, superw[pair]))
        if opening:
            in_team(1, first_product)
        else:
            in_team(1, lambda: spread(1))
            for block in (2 * pair - 2, 2 * pair - 1):
                lifting(child_block(block), block)
        drain_col(par, half)
    for ch in range(HALVES):
        child_pair(ch, PAIRS - 1)
    value = u_ref[PAIRS - 1]

    def lift_copy(at):
        return pltpu.make_async_remote_copy(
            src_ref=lift_buf.at[at, pl.ds(theirs, half)], dst_ref=lift_in.at[at],
            send_sem=lift_send.at[at], recv_sem=lift_recv.at[at],
            device_id=other, device_id_type=MESH,
        )

    for at in range(PAIRS):
        for side in range(2):
            lift_buf[at] += dot_t(
                value[:, side * WIDE:(side + 1) * WIDE],
                pair_rows(coupling, at, 2 * PAIRS - 2 + side),
            )
        lift_copy(at).start()

    def lift_ready(at):
        lift_copy(at).wait_recv()
        acc_r[at] = lift_buf[at, pl.ds(mine, half)] + lift_in[at]
        lift_copy(at).wait_send()

    lift_ready(0)

    def root_residual(pair, par):
        inverse_ready(PAIRS + pair)
        for ch in range(HALVES):
            rows = pl.ds(pl.multiple_of(mine + ch * fine, fine), fine)
            pending = root_rhs[pair, rows] - finish_col(ch, par, fine)
            start_row(ch, par, dot_n(pending, superw[PAIRS + pair]))

    for ch in range(HALVES):
        start_col(ch, 0, acc_r[0, root_rows[ch]])
    drain_row(1, half, 2 * WIDE)
    for at in range(1, PAIRS):
        lift_ready(at)
    root_residual(0, 0)
    gather_z(2)
    drain_col(0, fine)

    def root_forward(pair, carry):
        par = lax.rem(pair, 2)
        for ch in range(HALVES):
            value = finish_row(ch, 1 - par, fine, 2 * WIDE)
            v_ref[pair - 1, root_rows[ch]] = value
            for side in range(2):
                acc_r[pair, root_rows[ch]] += dot_t(
                    value[:, side * WIDE:(side + 1) * WIDE],
                    pair_rows(root_factor, pair, 2 * pair - 2 + side),
                )
            start_col(ch, par, acc_r[pair, root_rows[ch]])
        drain_row(1 - par, fine, 2 * WIDE)
        before = v_ref[pair - 1]

        @pl.loop(pair + 1, PAIRS)
        def _(later):
            for side in range(2):
                acc_r[later] += dot_t(
                    before[:, side * WIDE:(side + 1) * WIDE],
                    pair_rows(root_factor, later, 2 * pair - 2 + side),
                )

        root_residual(pair, par)
        pl.when(pair == 1)(lambda: in_team(2, gather_xy))
        pl.when(pair == 2)(lambda: in_team(2, first_product))
        pl.when(pair == 3)(lambda: in_team(2, second_product))
        drain_col(par, fine)
        return carry

    lax.fori_loop(1, PAIRS, root_forward, 0)

    def s_copy(pair):
        return pltpu.make_async_remote_copy(
            src_ref=s_half.at[pair], dst_ref=s_in.at[pair],
            send_sem=s_send.at[pair], recv_sem=s_recv.at[pair],
            device_id=other, device_id_type=MESH,
        )

    def root_solved(pair):
        s_copy(pair).wait_recv()
        root_out[pair, pl.ds(mine, half)] = s_half[pair]
        root_out[pair, pl.ds(theirs, half)] = s_in[pair]
        s_copy(pair).wait_send()

    def lower(value, pair, earlier):
        for side in range(2):
            acc_c[earlier, :, side * WIDE:(side + 1) * WIDE] += dot_n(
                value, pair_rows(coupling, pair, 2 * earlier + side)
            )

    for ch in range(HALVES):
        value = finish_row(ch, 1, fine, 2 * WIDE)
        v_ref[PAIRS - 1, root_rows[ch]] = value
        start_col(ch, 0, dot_t(value, superw[2 * PAIRS - 1]))
    in_team(2, lambda: spread(2))
    drain_row(1, fine, 2 * WIDE)

    def root_backward(step, carry):
        par = lax.rem(step, 2)
        pair = PAIRS - 1 - step
        after = pair + 1
        for ch in range(HALVES):
            rows = root_rows[ch]
            value = finish_col(ch, 1 - par, fine)
            s_half[after, rows] = value
            for side in range(2):
                acc_b[pair, rows, side * WIDE:(side + 1) * WIDE] += dot_n(
                    value, pair_rows(root_factor, after, 2 * pair + side)
                )
            start_row(ch, 1 - par, acc_b[pair, rows])
        s_copy(after).start()
        drain_col(1 - par, fine)
        solved = s_half[after]

        @pl.loop(0, pair)
        def _(earlier):
            for side in range(2):
                acc_b[earlier, :, side * WIDE:(side + 1) * WIDE] += dot_n(
                    solved, pair_rows(root_factor, after, 2 * earlier + side)
                )

        for ch in range(HALVES):
            pending = v_ref[pair, root_rows[ch]] - finish_row(ch, 1 - par, fine, 2 * WIDE)
            start_col(ch, par, dot_t(pending, superw[PAIRS + pair]))
        drain_row(1 - par, fine, 2 * WIDE)
        root_solved(after)
        both = root_out[after]

        @pl.loop(0, PAIRS)
        def _(earlier):
            lower(both, after, earlier)

        return carry

    lax.fori_loop(1, PAIRS, root_backward, 0)
    for ch in range(HALVES):
        s_half[0, root_rows[ch]] = finish_col(ch, 1, fine)
    s_copy(0).start()
    drain_col(1, fine)
    root_solved(0)

    last = root_out[0]
    lower(last, 0, PAIRS - 1)
    for ch in range(HALVES):
        start_row(ch, 1, acc_c[PAIRS - 1, child_rows[ch]])
    for earlier in range(PAIRS - 1):
        lower(last, 0, earlier)
    for at in range(SINGLES // 2):
        inverse_ready(at)

    def child_residual(pair, par):
        for ch in range(HALVES):
            pending = u_ref[pair, child_rows[ch]] - finish_row(ch, 1 - par, half, 2 * WIDE)
            start_col(ch, par, dot_t(pending, superw[pair]))
        drain_row(1 - par, half, 2 * WIDE)

    child_residual(PAIRS - 1, 0)

    def child_backward(step, carry):
        par = lax.rem(step, 2)
        pair = PAIRS - 1 - step
        after = pair + 1
        for ch in range(HALVES):
            rows = child_rows[ch]
            value = finish_col(ch, 1 - par, half)
            child_out[after, rows] = value
            for side in range(2):
                acc_c[pair, rows, side * WIDE:(side + 1) * WIDE] += dot_n(
                    value, pair_rows(child_factor, after, 2 * pair + side)
                )
            start_row(ch, 1 - par, acc_c[pair, rows])
        drain_col(1 - par, half)
        solved = child_out[after]

        @pl.loop(0, pair)
        def _(earlier):
            for side in range(2):
                acc_c[earlier, :, side * WIDE:(side + 1) * WIDE] += dot_n(
                    solved, pair_rows(child_factor, after, 2 * earlier + side)
                )

        child_residual(pair, par)
        for phase in range(3):
            @pl.when(step == phase + 1)
            def _():
                gather_z(phase, True)
                in_team(phase, lambda: spread(phase, True))

        return carry

    lax.fori_loop(1, PAIRS, child_backward, 0)
    for ch in range(HALVES):
        child_out[0, child_rows[ch]] = finish_col(ch, 1, half)
    drain_col(1, half)


def paired(x):
    return jnp.transpose(x.reshape(x.shape[0], PAIRS, 2 * THIN), (1, 0, 2))


def unpaired(x):
    return jnp.transpose(x, (1, 0, 2)).reshape(x.shape[1], 2 * PAIRS, THIN)


def local(root_rhs, child_rhs, root_factor, child_factor, coupling, root_inverse, child_inverse):
    nrhs = root_rhs.shape[0]
    half = nrhs // 2
    vmem = pl.BlockSpec(memory_space=pltpu.VMEM)
    f32 = jnp.float32
    dma = pltpu.SemaphoreType.DMA
    root, child = pl.pallas_call(
        kernel,
        out_shape=(
            jax.ShapeDtypeStruct((PAIRS, nrhs, 2 * THIN), f32),
            jax.ShapeDtypeStruct((PAIRS, nrhs, 2 * THIN), f32),
        ),
        in_specs=[vmem] * 2 + [pl.BlockSpec(memory_space=pltpu.HBM)] * 5,
        out_specs=[vmem] * 2,
        scratch_shapes=[
            pltpu.VMEM(root_factor.shape, f32),
            pltpu.VMEM(root_factor.shape, f32),
            pltpu.VMEM(root_factor.shape, f32),
            pltpu.VMEM((2 * PAIRS, THIN, WIDE), f32),
            pltpu.VMEM((2 * PAIRS, THIN, WIDE), f32),
            pltpu.VMEM((PAIRS, nrhs, 2 * WIDE), f32),
            pltpu.VMEM((PAIRS, half, 2 * WIDE), f32),
            pltpu.VMEM((PAIRS, half, 2 * THIN), f32),
            pltpu.VMEM((PAIRS, half, 2 * THIN), f32),
            pltpu.VMEM((PAIRS, nrhs, 2 * THIN), f32),
            pltpu.VMEM((PAIRS, half, 2 * THIN), f32),
            pltpu.VMEM((PAIRS, half, 2 * WIDE), f32),
            pltpu.VMEM((PAIRS, nrhs, 2 * WIDE), f32),
            pltpu.VMEM((2 * PAIRS, 2 * THIN, 2 * WIDE), f32),
            pltpu.VMEM((HALVES, 2, COLS, half, 2 * THIN), f32),
            pltpu.VMEM((HALVES, 2, ROWS, half, 2 * WIDE), f32),
            pltpu.VMEM((PAIRS, nrhs, 2 * THIN), f32),
            pltpu.VMEM((PAIRS, half, 2 * THIN), f32),
            pltpu.VMEM((4, COLS, THIN, WIDE), f32),
            pltpu.VMEM((4, COLS, THIN, WIDE), f32),
            pltpu.VMEM((4, COLS, THIN, WIDE), f32),
            pltpu.VMEM((4 * THIN, 4 * THIN), f32),
            pltpu.VMEM((COLS, 4 * THIN, WIDE), f32),
            pltpu.VMEM((4, 2, 4 * THIN, WIDE), f32),
            pltpu.VMEM((2, 4 * THIN, WIDE), f32),
            dma((HALVES, 2, COLS)), dma((HALVES, 2, COLS)),
            dma((HALVES, 2, ROWS)), dma((HALVES, 2, ROWS)),
            dma((PAIRS,)), dma((PAIRS,)), dma((PAIRS,)), dma((PAIRS,)),
            dma((3, 2, 3)), dma((3,)), dma((4, 4)), dma((4, 4)),
            dma((2, 2, 4)), dma((2 * PAIRS,)), dma((5,)),
        ],
        compiler_params=pltpu.CompilerParams(
            collective_id=0, has_side_effects=True, vmem_limit_bytes=48 << 20
        ),
    )(
        paired(root_rhs), paired(child_rhs[0]),
        root_factor, child_factor[0], coupling[0],
        jnp.swapaxes(root_inverse, 1, 2), jnp.swapaxes(child_inverse[0], 1, 2),
    )
    return unpaired(root), unpaired(child)[None]


def solution(mesh):
    in_specs = (
        P(None, None, "row"),
        P("layer", None, None, "row"),
        P(None, None, "row", "col"),
        P("layer", None, None, "row", "col"),
        P("layer", None, None, "row", "col"),
        P(None, "col", "row"),
        P("layer", None, "col", "row"),
    )
    out_specs = (P(None, None, "row"), P("layer", None, None, "row"))
    return jax.shard_map(local, mesh=mesh, in_specs=in_specs, out_specs=out_specs, check_vma=False)
```

```python
import jax
import jax.numpy as jnp
from jax import lax
from jax.experimental import pallas as pl
from jax.experimental.pallas import tpu as pltpu
from jax.sharding import PartitionSpec as P

MESH = pl.DeviceIdType.MESH
PAIRS = 4
ROWS = 16
COLS = 8
THIN = 64
WIDE = 128
SINGLES = 4
HALVES = 2


def dot_t(x, y):
    return lax.dot_general(
        x, y, (((1,), (1,)), ((), ())), precision=lax.Precision.HIGHEST,
        preferred_element_type=jnp.float32,
    )


def dot_n(x, y):
    return lax.dot_general(
        x, y, (((1,), (0,)), ((), ())), precision=lax.Precision.HIGHEST,
        preferred_element_type=jnp.float32,
    )


def pack(x):
    half = x.shape[0] // 2
    return jnp.concatenate([x[:half], x[half:]], axis=1)


def unpack(x):
    half = x.shape[1] // 2
    return jnp.concatenate([x[:, :half], x[:, half:]], axis=0)


def pair_rows(ref, pair, block):
    return ref[pl.ds(2 * pair, 2), block].reshape(2 * THIN, WIDE)


def kernel(
    root_rhs_in, child_rhs_in, root_factor_hbm, child_factor_hbm, coupling_hbm, root_wt_hbm,
    child_wt_hbm,
    root_result, child_result,
    root_rhs, child_rhs, root_out, child_out,
    root_factor, child_factor, coupling, root_wt, child_wt,
    u_ref, v_ref, s_half, s_in, acc_f, acc_r, acc_b, acc_c, superw,
    col_buf, row_buf, lift_buf, lift_in, a0_buf, c_buf, a1_buf, t_buf, x_out, x_in, x_buf,
    col_send, col_recv, row_send, row_recv, lift_send, lift_recv, s_send, s_recv,
    z_send, z_recv, xy_send, xy_recv, x_send, x_recv, in_sem,
):
    layer = lax.axis_index("layer")
    row = lax.axis_index("row")
    col = lax.axis_index("col")
    other = (1 - layer, row, col)
    col_peers = [lax.rem(col + k, COLS) for k in range(1, COLS)]
    row_peers = [lax.rem(row + k, ROWS) for k in range(1, ROWS)]
    row4, rowm = row // 4, lax.rem(row, 4)
    col2, colm = col // 2, lax.rem(col, 2)
    nrhs = child_rhs.shape[1]
    half = nrhs // 2
    mine = pl.multiple_of(layer * half, half)
    theirs = pl.multiple_of((1 - layer) * half, half)

    loads = [
        pltpu.make_async_copy(src, dst, in_sem.at[at])
        for at, (src, dst) in enumerate((
            (child_wt_hbm, child_wt), (child_factor_hbm, child_factor),
            (coupling_hbm, coupling), (root_wt_hbm, root_wt), (root_factor_hbm, root_factor),
        ))
    ]
    for load in loads:
        load.start()
    barrier = pltpu.get_barrier_semaphore()
    for peer in col_peers:
        pl.semaphore_signal(barrier, inc=1, device_id=(layer, row, peer), device_id_type=MESH)
    for peer in row_peers:
        pl.semaphore_signal(barrier, inc=1, device_id=(layer, peer, col), device_id_type=MESH)
    pl.semaphore_signal(barrier, inc=1, device_id=other, device_id_type=MESH)
    for block in range(2 * PAIRS):
        at = (block // 2, slice(None), slice((block % 2) * THIN, (block % 2 + 1) * THIN))
        child_rhs[at] = child_rhs_in[:, block]
        root_rhs[at] = root_rhs_in[:, block]
    for ref in (acc_f, acc_b, acc_c, lift_buf):
        ref[...] = jnp.zeros_like(ref)
    pl.semaphore_wait(barrier, COLS + ROWS - 1)

    def col_copy(ch, par, slot, at, height, peer):
        where = col_buf.at[ch, par, slot, pl.ds(0, height)]
        return pltpu.make_async_remote_copy(
            src_ref=where, dst_ref=where,
            send_sem=col_send.at[ch, par, at], recv_sem=col_recv.at[ch, par, slot],
            device_id=(layer, row, peer), device_id_type=MESH,
        )

    def row_copy(ch, par, slot, at, height, width, peer):
        where = row_buf.at[ch, par, slot, pl.ds(0, height), pl.ds(0, width)]
        return pltpu.make_async_remote_copy(
            src_ref=where, dst_ref=where,
            send_sem=row_send.at[ch, par, at], recv_sem=row_recv.at[ch, par, slot],
            device_id=(layer, peer, col), device_id_type=MESH,
        )

    def start_col(ch, par, value):
        height = value.shape[0]
        col_buf[ch, par, col, 0:height] = value
        for at, peer in enumerate(col_peers):
            col_copy(ch, par, col, at, height, peer).start()

    def finish_col(ch, par, height):
        for at, peer in enumerate(col_peers):
            col_copy(ch, par, peer, at, height, peer).wait_recv()
        total = col_buf[ch, par, 0, 0:height]
        for slot in range(1, COLS):
            total = total + col_buf[ch, par, slot, 0:height]
        return total

    def drain_col(par, height):
        for ch in range(HALVES):
            for at, peer in enumerate(col_peers):
                col_copy(ch, par, col, at, height, peer).wait_send()

    def start_row(ch, par, value):
        height, width = value.shape
        row_buf[ch, par, row, 0:height, 0:width] = value
        for at, peer in enumerate(row_peers):
            row_copy(ch, par, row, at, height, width, peer).start()

    def finish_row(ch, par, height, width):
        for at, peer in enumerate(row_peers):
            row_copy(ch, par, peer, at, height, width, peer).wait_recv()
        total = row_buf[ch, par, 0, 0:height, 0:width]
        for slot in range(1, ROWS):
            total = total + row_buf[ch, par, slot, 0:height, 0:width]
        return total

    def drain_row(par, height, width):
        for ch in range(HALVES):
            for at, peer in enumerate(row_peers):
                row_copy(ch, par, row, at, height, width, peer).wait_send()

    phases = (
        (0, 2, child_wt, child_factor, 2),
        (2, 2 * layer, root_wt, root_factor, PAIRS + 2 * layer),
        (1, 0, child_wt, child_factor, 0),
    )

    def placed(src, dst, recv, send, to_layer, to_row, to_col, wanted, finish):
        here = jnp.logical_and(
            to_layer == layer, jnp.logical_and(to_row == row, to_col == col)
        )

        @pl.when(jnp.logical_and(wanted, jnp.logical_not(here)))
        def _():
            copy = pltpu.make_async_remote_copy(
                src_ref=src, dst_ref=dst, send_sem=send, recv_sem=recv,
                device_id=(to_layer, to_row, to_col), device_id_type=MESH,
            )
            copy.wait_send() if finish else copy.start()

        if not finish:
            @pl.when(jnp.logical_and(wanted, here))
            def _():
                pltpu.make_async_copy(src, dst, recv).start()

    def arrived(ref, sem):
        pltpu.make_async_copy(ref, ref, sem).wait()

    def gather_z(phase, finish=False):
        base, first, wt, factor, _ = phases[phase]
        for which in range(2):
            pair, team = first + which, base + 4 * which
            needed = col2 >= row4
            for kind, (src, dst, wanted) in enumerate((
                (wt.at[2 * pair], a0_buf.at[rowm, col], needed),
                (factor.at[2 * pair + 1, 2 * pair], c_buf.at[row4, col], True),
                (wt.at[2 * pair + 1], a1_buf.at[row4, col], needed),
            )):
                placed(
                    src, dst, z_recv.at[kind], z_send.at[phase, which, kind],
                    layer, row, team, wanted, finish,
                )

    def team_copy(src, dst, send, recv, to_row):
        return pltpu.make_async_remote_copy(
            src_ref=src, dst_ref=dst, send_sem=send, recv_sem=recv,
            device_id=(layer, to_row, col), device_id_type=MESH,
        )

    def tail(ref, slot, part):
        return ref.at[slot, pl.ds(2 * part, COLS - 2 * part)]

    def a0_copy(part, slot, to):
        where = tail(a0_buf, slot, part)
        return team_copy(where, where, xy_send.at[0, to], xy_recv.at[0, slot], 4 * row4 + to)

    def c_copy(part, slot, to):
        where = tail(c_buf, slot, part)
        return team_copy(where, where, xy_send.at[1, to], xy_recv.at[1, slot], 4 * to + rowm)

    def a1_copy(part, slot, to):
        where = tail(a1_buf, slot, part)
        return team_copy(where, where, xy_send.at[2, to], xy_recv.at[2, slot], 4 * to + rowm)

    def part_copy(slot, to):
        return team_copy(
            x_out.at[pl.ds(2 * to, 2)], x_in.at[slot],
            xy_send.at[3, to], xy_recv.at[3, slot], 4 * row4 + to,
        )

    def in_team(phase, work):
        pl.when(lax.rem(col, 4) == phases[phase][0])(work)

    def gather_ac():
        arrived(c_buf.at[row4], z_recv.at[1])
        for to in range(4):
            @pl.when(row4 != to)
            def _():
                c_copy(to, row4, to).start()
        for part in range(4):
            @pl.when(row4 == part)
            def _():
                arrived(tail(a0_buf, rowm, part), z_recv.at[0])
                for to in range(4):
                    @pl.when(rowm != to)
                    def _():
                        a0_copy(part, rowm, to).start()

    def gather_a1():
        for part in range(4):
            @pl.when(row4 == part)
            def _():
                arrived(tail(a1_buf, row4, part), z_recv.at[2])
                for to in range(4):
                    if to != part:
                        a1_copy(part, row4, to).start()

    def first_product():
        for part in range(4):
            @pl.when(row4 == part)
            def _():
                for slot in range(4):
                    @pl.when(rowm != slot)
                    def _():
                        a0_copy(part, slot, slot).wait_recv()
                    if slot != part:
                        c_copy(part, slot, slot).wait_recv()
        t_buf[...] = jnp.zeros_like(t_buf)

        @pl.loop(2 * row4, COLS)
        def _(at):
            t_buf[...] += dot_t(
                a0_buf[:, at].reshape(4 * THIN, WIDE), c_buf[:, at].reshape(4 * THIN, WIDE)
            )

    def second_product():
        for slot in range(4):
            @pl.when(row4 != slot)
            def _():
                a1_copy(slot, slot, slot).wait_recv()
        for at in range(COLS):
            deep = at // 2 + 1
            x_out[at] = dot_n(
                t_buf[:, 0:deep * THIN], a1_buf[0:deep, at].reshape(deep * THIN, WIDE)
            )

    def send_parts():
        for to in range(4):
            @pl.when(rowm != to)
            def _():
                part_copy(rowm, to).start()

    def spread(phase, finish=False):
        if finish:
            for part in range(4):
                @pl.when(row4 == part)
                def _():
                    for to in range(4):
                        @pl.when(rowm != to)
                        def _():
                            a0_copy(part, rowm, to).wait_send()
                        if to != part:
                            a1_copy(part, row4, to).wait_send()
            for to in range(4):
                @pl.when(row4 != to)
                def _():
                    c_copy(to, row4, to).wait_send()
                @pl.when(rowm != to)
                def _():
                    part_copy(rowm, to).wait_send()
        else:
            x_in[rowm] = x_out[pl.ds(2 * rowm, 2)]
            for slot in range(4):
                @pl.when(rowm != slot)
                def _():
                    part_copy(slot, slot).wait_recv()
            for side in range(2):
                x_buf[side] = -(
                    (x_in[0, side] + x_in[1, side]) + (x_in[2, side] + x_in[3, side])
                )
        slot = phases[phase][4] + col // 4
        for to in range(2):
            if phase != 1 and to == 1:
                continue
            for side in range(2):
                for part in range(4):
                    placed(
                        x_buf.at[side, pl.ds(part * THIN, THIN)],
                        superw.at[slot, pl.ds(0, THIN), pl.ds(WIDE, WIDE)],
                        x_recv.at[slot], x_send.at[to, side, part],
                        layer if to == 0 else 1 - layer,
                        4 * row4 + part, 2 * rowm + side, True, finish,
                    )

    def inverse_ready(at):
        arrived(superw.at[at, pl.ds(0, THIN), pl.ds(WIDE, WIDE)], x_recv.at[at])

    def fill_superw():
        for base, wt in ((0, child_wt), (PAIRS, root_wt)):
            for pair in range(PAIRS):
                superw[base + pair, 0:THIN, 0:WIDE] = wt[2 * pair]
                superw[base + pair, THIN:, WIDE:] = wt[2 * pair + 1]
                superw[base + pair, THIN:, 0:WIDE] = jnp.zeros((THIN, WIDE), jnp.float32)

    def child_trailing(value, block, first):
        for later in range(first, PAIRS):
            acc_f[later] += dot_t(value, pair_rows(child_factor, later, block))

    def lifting(value, block):
        for at in range(PAIRS):
            lift_buf[at] += dot_t(value, pair_rows(coupling, at, block))

    fine = half // HALVES
    child_rows = [slice(ch * half, (ch + 1) * half) for ch in range(HALVES)]
    root_rows = [slice(ch * fine, (ch + 1) * fine) for ch in range(HALVES)]

    def child_value(ch, block):
        value = finish_row(ch, block % 2, half, WIDE)
        rows, pair, side = child_rows[ch], block // 2, block % 2
        u_ref[pair, rows, side * WIDE:(side + 1) * WIDE] = value
        if side == 0:
            acc_f[pair, rows, THIN:] += dot_t(value, child_factor[block + 1, block])
        else:
            acc_f[pair + 1, rows] += dot_t(value, pair_rows(child_factor, pair + 1, block))

    def child_block(block):
        return u_ref[block // 2, :, (block % 2) * WIDE:(block % 2 + 1) * WIDE]

    loads[0].wait()
    for ch in range(HALVES):
        start_row(ch, 0, dot_n(child_rhs[0, child_rows[ch], 0:THIN], child_wt[0]))
    for load in loads[1:]:
        load.wait()
    gather_z(0)
    gather_z(1)
    fill_superw()
    for block in range(1, SINGLES):
        par = block % 2
        pair, side = block // 2, block % 2
        low, high = side * THIN, (side + 1) * THIN
        for ch in range(HALVES):
            child_value(ch, block - 1)
            start_col(ch, par, pack(acc_f[pair, child_rows[ch], low:high]))
        for phase in range(2):
            if block == 1:
                in_team(phase, gather_ac)
            if block == 2:
                in_team(phase, gather_a1)
                in_team(phase, first_product)
            if block == 3:
                in_team(phase, lambda: spread(phase))
        drain_row(1 - par, half, WIDE)
        child_trailing(child_block(block - 1), block - 1, pair + 1)
        for ch in range(HALVES):
            total = unpack(finish_col(ch, par, half // 2))
            pending = child_rhs[pair, child_rows[ch], low:high] - total
            start_row(ch, par, dot_n(pending, child_wt[block]))
        for phase in range(2):
            if block == 2:
                in_team(phase, second_product)
                in_team(phase, send_parts)
        drain_col(par, half // 2)
        lifting(child_block(block - 1), block - 1)

    def child_pair(ch, pair):
        value = finish_row(ch, pair % 2, half, 2 * WIDE)
        rows = child_rows[ch]
        u_ref[pair, rows] = value
        if pair + 1 < PAIRS:
            for side in range(2):
                acc_f[pair + 1, rows] += dot_t(
                    value[:, side * WIDE:(side + 1) * WIDE],
                    pair_rows(child_factor, pair + 1, 2 * pair + side),
                )

    for pair in range(SINGLES // 2, PAIRS):
        par = pair % 2
        opening = pair == SINGLES // 2
        for ch in range(HALVES):
            if opening:
                child_value(ch, SINGLES - 1)
            else:
                child_pair(ch, pair - 1)
            start_col(ch, par, acc_f[pair, child_rows[ch]])
        if opening:
            drain_row(1 - par, half, WIDE)
            child_trailing(child_block(SINGLES - 1), SINGLES - 1, pair + 1)
            lifting(child_block(SINGLES - 1), SINGLES - 1)
        else:
            drain_row(1 - par, half, 2 * WIDE)
            for block in (2 * pair - 2, 2 * pair - 1):
                child_trailing(child_block(block), block, pair + 1)
        inverse_ready(pair)
        for ch in range(HALVES):
            pending = child_rhs[pair, child_rows[ch]] - finish_col(ch, par, half)
            start_row(ch, par, dot_n(pending, superw[pair]))
        if not opening:
            for block in (2 * pair - 2, 2 * pair - 1):
                lifting(child_block(block), block)
        drain_col(par, half)
    for ch in range(HALVES):
        child_pair(ch, PAIRS - 1)
    value = u_ref[PAIRS - 1]

    def lift_copy(at):
        return pltpu.make_async_remote_copy(
            src_ref=lift_buf.at[at, pl.ds(theirs, half)], dst_ref=lift_in.at[at],
            send_sem=lift_send.at[at], recv_sem=lift_recv.at[at],
            device_id=other, device_id_type=MESH,
        )

    for at in range(PAIRS):
        for side in range(2):
            lift_buf[at] += dot_t(
                value[:, side * WIDE:(side + 1) * WIDE],
                pair_rows(coupling, at, 2 * PAIRS - 2 + side),
            )
        lift_copy(at).start()

    def lift_ready(at):
        lift_copy(at).wait_recv()
        acc_r[at] = lift_buf[at, pl.ds(mine, half)] + lift_in[at]
        lift_copy(at).wait_send()

    lift_ready(0)

    def root_residual(pair, par):
        inverse_ready(PAIRS + pair)
        for ch in range(HALVES):
            rows = pl.ds(pl.multiple_of(mine + ch * fine, fine), fine)
            pending = root_rhs[pair, rows] - finish_col(ch, par, fine)
            start_row(ch, par, dot_n(pending, superw[PAIRS + pair]))

    for ch in range(HALVES):
        start_col(ch, 0, acc_r[0, root_rows[ch]])
    drain_row(1, half, 2 * WIDE)
    for at in range(1, PAIRS):
        lift_ready(at)
    root_residual(0, 0)
    gather_z(2)
    drain_col(0, fine)

    def root_forward(pair, carry):
        par = lax.rem(pair, 2)
        for ch in range(HALVES):
            value = finish_row(ch, 1 - par, fine, 2 * WIDE)
            v_ref[pair - 1, root_rows[ch]] = value
            for side in range(2):
                acc_r[pair, root_rows[ch]] += dot_t(
                    value[:, side * WIDE:(side + 1) * WIDE],
                    pair_rows(root_factor, pair, 2 * pair - 2 + side),
                )
            start_col(ch, par, acc_r[pair, root_rows[ch]])
        pl.when(pair == 1)(lambda: in_team(2, gather_ac))
        pl.when(pair == 2)(lambda: in_team(2, gather_a1))
        pl.when(pair == 3)(lambda: in_team(2, send_parts))
        drain_row(1 - par, fine, 2 * WIDE)
        before = v_ref[pair - 1]

        @pl.loop(pair + 1, PAIRS)
        def _(later):
            for side in range(2):
                acc_r[later] += dot_t(
                    before[:, side * WIDE:(side + 1) * WIDE],
                    pair_rows(root_factor, later, 2 * pair - 2 + side),
                )

        root_residual(pair, par)
        pl.when(pair == 1)(lambda: in_team(2, first_product))
        pl.when(pair == 2)(lambda: in_team(2, second_product))
        pl.when(pair == 3)(lambda: in_team(2, lambda: spread(2)))
        drain_col(par, fine)
        return carry

    lax.fori_loop(1, PAIRS, root_forward, 0)

    def s_copy(pair):
        return pltpu.make_async_remote_copy(
            src_ref=s_half.at[pair], dst_ref=s_in.at[pair],
            send_sem=s_send.at[pair], recv_sem=s_recv.at[pair],
            device_id=other, device_id_type=MESH,
        )

    def root_solved(pair):
        s_copy(pair).wait_recv()
        root_out[pair, pl.ds(mine, half)] = s_half[pair]
        root_out[pair, pl.ds(theirs, half)] = s_in[pair]
        s_copy(pair).wait_send()

    def lower(value, pair, earlier):
        for side in range(2):
            acc_c[earlier, :, side * WIDE:(side + 1) * WIDE] += dot_n(
                value, pair_rows(coupling, pair, 2 * earlier + side)
            )

    for ch in range(HALVES):
        value = finish_row(ch, 1, fine, 2 * WIDE)
        v_ref[PAIRS - 1, root_rows[ch]] = value
        start_col(ch, 0, dot_t(value, superw[2 * PAIRS - 1]))
    drain_row(1, fine, 2 * WIDE)

    def root_backward(step, carry):
        par = lax.rem(step, 2)
        pair = PAIRS - 1 - step
        after = pair + 1
        for ch in range(HALVES):
            rows = root_rows[ch]
            value = finish_col(ch, 1 - par, fine)
            s_half[after, rows] = value
            for side in range(2):
                acc_b[pair, rows, side * WIDE:(side + 1) * WIDE] += dot_n(
                    value, pair_rows(root_factor, after, 2 * pair + side)
                )
            start_row(ch, 1 - par, acc_b[pair, rows])
        s_copy(after).start()
        drain_col(1 - par, fine)
        solved = s_half[after]

        @pl.loop(0, pair)
        def _(earlier):
            for side in range(2):
                acc_b[earlier, :, side * WIDE:(side + 1) * WIDE] += dot_n(
                    solved, pair_rows(root_factor, after, 2 * earlier + side)
                )

        for ch in range(HALVES):
            pending = v_ref[pair, root_rows[ch]] - finish_row(ch, 1 - par, fine, 2 * WIDE)
            start_col(ch, par, dot_t(pending, superw[PAIRS + pair]))
        drain_row(1 - par, fine, 2 * WIDE)
        root_solved(after)
        both = root_out[after]

        @pl.loop(0, PAIRS)
        def _(earlier):
            lower(both, after, earlier)

        return carry

    lax.fori_loop(1, PAIRS, root_backward, 0)
    for ch in range(HALVES):
        s_half[0, root_rows[ch]] = finish_col(ch, 1, fine)
    s_copy(0).start()
    drain_col(1, fine)
    root_solved(0)

    last = root_out[0]
    lower(last, 0, PAIRS - 1)
    for ch in range(HALVES):
        start_row(ch, 1, acc_c[PAIRS - 1, child_rows[ch]])
    for earlier in range(PAIRS - 1):
        lower(last, 0, earlier)
    for at in range(SINGLES // 2):
        inverse_ready(at)

    def child_residual(pair, par):
        for ch in range(HALVES):
            pending = u_ref[pair, child_rows[ch]] - finish_row(ch, 1 - par, half, 2 * WIDE)
            start_col(ch, par, dot_t(pending, superw[pair]))
        drain_row(1 - par, half, 2 * WIDE)

    child_residual(PAIRS - 1, 0)

    def write_pair(result, source, pair):
        for side in range(2):
            result[:, 2 * pair + side] = source[pair, :, side * THIN:(side + 1) * THIN]

    for pair in range(PAIRS):
        write_pair(root_result, root_out, pair)

    def child_backward(step, carry):
        par = lax.rem(step, 2)
        pair = PAIRS - 1 - step
        after = pair + 1
        for ch in range(HALVES):
            rows = child_rows[ch]
            value = finish_col(ch, 1 - par, half)
            child_out[after, rows] = value
            for side in range(2):
                acc_c[pair, rows, side * WIDE:(side + 1) * WIDE] += dot_n(
                    value, pair_rows(child_factor, after, 2 * pair + side)
                )
            start_row(ch, 1 - par, acc_c[pair, rows])
        drain_col(1 - par, half)
        solved = child_out[after]

        @pl.loop(0, pair)
        def _(earlier):
            for side in range(2):
                acc_c[earlier, :, side * WIDE:(side + 1) * WIDE] += dot_n(
                    solved, pair_rows(child_factor, after, 2 * earlier + side)
                )

        child_residual(pair, par)
        for phase in range(3):
            @pl.when(step == phase + 1)
            def _():
                gather_z(phase, True)
                in_team(phase, lambda: spread(phase, True))

        return carry

    lax.fori_loop(1, PAIRS, child_backward, 0)
    for ch in range(HALVES):
        child_out[0, child_rows[ch]] = finish_col(ch, 1, half)
    for pair in range(PAIRS):
        write_pair(child_result, child_out, pair)
    drain_col(1, half)


def local(root_rhs, child_rhs, root_factor, child_factor, coupling, root_inverse, child_inverse):
    nrhs = root_rhs.shape[0]
    half = nrhs // 2
    vmem = pl.BlockSpec(memory_space=pltpu.VMEM)
    f32 = jnp.float32
    dma = pltpu.SemaphoreType.DMA
    root, child = pl.pallas_call(
        kernel,
        out_shape=(
            jax.ShapeDtypeStruct((nrhs, 2 * PAIRS, THIN), f32),
            jax.ShapeDtypeStruct((nrhs, 2 * PAIRS, THIN), f32),
        ),
        in_specs=[vmem] * 2 + [pl.BlockSpec(memory_space=pltpu.HBM)] * 5,
        out_specs=[vmem] * 2,
        scratch_shapes=[
            pltpu.VMEM((PAIRS, nrhs, 2 * THIN), f32),
            pltpu.VMEM((PAIRS, nrhs, 2 * THIN), f32),
            pltpu.VMEM((PAIRS, nrhs, 2 * THIN), f32),
            pltpu.VMEM((PAIRS, nrhs, 2 * THIN), f32),
            pltpu.VMEM(root_factor.shape, f32),
            pltpu.VMEM(root_factor.shape, f32),
            pltpu.VMEM(root_factor.shape, f32),
            pltpu.VMEM((2 * PAIRS, THIN, WIDE), f32),
            pltpu.VMEM((2 * PAIRS, THIN, WIDE), f32),
            pltpu.VMEM((PAIRS, nrhs, 2 * WIDE), f32),
            pltpu.VMEM((PAIRS, half, 2 * WIDE), f32),
            pltpu.VMEM((PAIRS, half, 2 * THIN), f32),
            pltpu.VMEM((PAIRS, half, 2 * THIN), f32),
            pltpu.VMEM((PAIRS, nrhs, 2 * THIN), f32),
            pltpu.VMEM((PAIRS, half, 2 * THIN), f32),
            pltpu.VMEM((PAIRS, half, 2 * WIDE), f32),
            pltpu.VMEM((PAIRS, nrhs, 2 * WIDE), f32),
            pltpu.VMEM((2 * PAIRS, 2 * THIN, 2 * WIDE), f32),
            pltpu.VMEM((HALVES, 2, COLS, half, 2 * THIN), f32),
            pltpu.VMEM((HALVES, 2, ROWS, half, 2 * WIDE), f32),
            pltpu.VMEM((PAIRS, nrhs, 2 * THIN), f32),
            pltpu.VMEM((PAIRS, half, 2 * THIN), f32),
            pltpu.VMEM((4, COLS, THIN, WIDE), f32),
            pltpu.VMEM((4, COLS, THIN, WIDE), f32),
            pltpu.VMEM((4, COLS, THIN, WIDE), f32),
            pltpu.VMEM((4 * THIN, 4 * THIN), f32),
            pltpu.VMEM((COLS, 4 * THIN, WIDE), f32),
            pltpu.VMEM((4, 2, 4 * THIN, WIDE), f32),
            pltpu.VMEM((2, 4 * THIN, WIDE), f32),
            dma((HALVES, 2, COLS)), dma((HALVES, 2, COLS)),
            dma((HALVES, 2, ROWS)), dma((HALVES, 2, ROWS)),
            dma((PAIRS,)), dma((PAIRS,)), dma((PAIRS,)), dma((PAIRS,)),
            dma((3, 2, 3)), dma((3,)), dma((4, 4)), dma((4, 4)),
            dma((2, 2, 4)), dma((2 * PAIRS,)), dma((5,)),
        ],
        compiler_params=pltpu.CompilerParams(
            collective_id=0, has_side_effects=True, vmem_limit_bytes=60 << 20
        ),
    )(
        root_rhs, child_rhs[0],
        root_factor, child_factor[0], coupling[0],
        jnp.swapaxes(root_inverse, 1, 2), jnp.swapaxes(child_inverse[0], 1, 2),
    )
    return root, child[None]


def solution(mesh):
    in_specs = (
        P(None, None, "row"),
        P("layer", None, None, "row"),
        P(None, None, "row", "col"),
        P("layer", None, None, "row", "col"),
        P("layer", None, None, "row", "col"),
        P(None, "col", "row"),
        P("layer", None, "col", "row"),
    )
    out_specs = (P(None, None, "row"), P("layer", None, None, "row"))
    return jax.shard_map(local, mesh=mesh, in_specs=in_specs, out_specs=out_specs, check_vma=False)
```

```python
import jax
import jax.numpy as jnp
from jax import lax
from jax.experimental import pallas as pl
from jax.experimental.pallas import tpu as pltpu
from jax.sharding import PartitionSpec as P

MESH = pl.DeviceIdType.MESH
PAIRS = 4
ROWS = 16
COLS = 8
THIN = 64
WIDE = 128
SINGLES = 4
HALVES = 2


def halves(x):
    high = x.astype(jnp.bfloat16)
    return high, (x - high.astype(jnp.float32)).astype(jnp.bfloat16)


def product(x, y, dims):
    (x_high, x_low), (y_high, y_low) = halves(x), halves(y)

    def one(left, right):
        return lax.dot_general(left, right, (dims, ((), ())), preferred_element_type=jnp.float32)

    return one(x_high, y_high) + (one(x_high, y_low) + one(x_low, y_high))


def dot_t(x, y):
    return product(x, y, ((1,), (1,)))


def dot_n(x, y):
    return product(x, y, ((1,), (0,)))


def pack(x):
    half = x.shape[0] // 2
    return jnp.concatenate([x[:half], x[half:]], axis=1)


def unpack(x):
    half = x.shape[1] // 2
    return jnp.concatenate([x[:, :half], x[:, half:]], axis=0)


def pair_rows(ref, pair, block):
    return ref[pl.ds(2 * pair, 2), block].reshape(2 * THIN, WIDE)


def kernel(
    root_rhs_in, child_rhs_in, root_factor_hbm, child_factor_hbm, coupling_hbm, root_wt_hbm,
    child_wt_hbm,
    root_result, child_result,
    root_rhs, child_rhs, root_out, child_out,
    root_factor, child_factor, coupling, root_wt, child_wt,
    u_ref, v_ref, s_half, s_in, acc_f, acc_r, acc_b, acc_c, superw,
    col_buf, row_buf, lift_buf, lift_in, a0_buf, c_buf, a1_buf, t_buf, x_out, x_in, x_buf,
    col_send, col_recv, row_send, row_recv, lift_send, lift_recv, s_send, s_recv,
    z_send, z_recv, xy_send, xy_recv, x_send, x_recv, in_sem,
):
    layer = lax.axis_index("layer")
    row = lax.axis_index("row")
    col = lax.axis_index("col")
    other = (1 - layer, row, col)
    col_peers = [lax.rem(col + k, COLS) for k in range(1, COLS)]
    row_peers = [lax.rem(row + k, ROWS) for k in range(1, ROWS)]
    row4, rowm = row // 4, lax.rem(row, 4)
    col2, colm = col // 2, lax.rem(col, 2)
    nrhs = child_rhs.shape[1]
    half = nrhs // 2
    mine = pl.multiple_of(layer * half, half)
    theirs = pl.multiple_of((1 - layer) * half, half)

    loads = [
        pltpu.make_async_copy(src, dst, in_sem.at[at])
        for at, (src, dst) in enumerate((
            (child_wt_hbm, child_wt), (child_factor_hbm, child_factor),
            (coupling_hbm, coupling), (root_wt_hbm, root_wt), (root_factor_hbm, root_factor),
        ))
    ]
    for load in loads:
        load.start()
    barrier = pltpu.get_barrier_semaphore()
    for peer in col_peers:
        pl.semaphore_signal(barrier, inc=1, device_id=(layer, row, peer), device_id_type=MESH)
    for peer in row_peers:
        pl.semaphore_signal(barrier, inc=1, device_id=(layer, peer, col), device_id_type=MESH)
    pl.semaphore_signal(barrier, inc=1, device_id=other, device_id_type=MESH)
    for block in range(2 * PAIRS):
        at = (block // 2, slice(None), slice((block % 2) * THIN, (block % 2 + 1) * THIN))
        child_rhs[at] = child_rhs_in[:, block]
        root_rhs[at] = root_rhs_in[:, block]
    for ref in (acc_f, acc_b, acc_c, lift_buf):
        ref[...] = jnp.zeros_like(ref)
    pl.semaphore_wait(barrier, COLS + ROWS - 1)

    def col_copy(ch, par, slot, at, height, peer):
        where = col_buf.at[ch, par, slot, pl.ds(0, height)]
        return pltpu.make_async_remote_copy(
            src_ref=where, dst_ref=where,
            send_sem=col_send.at[ch, par, at], recv_sem=col_recv.at[ch, par, slot],
            device_id=(layer, row, peer), device_id_type=MESH,
        )

    def row_copy(ch, par, slot, at, height, width, peer):
        where = row_buf.at[ch, par, slot, pl.ds(0, height), pl.ds(0, width)]
        return pltpu.make_async_remote_copy(
            src_ref=where, dst_ref=where,
            send_sem=row_send.at[ch, par, at], recv_sem=row_recv.at[ch, par, slot],
            device_id=(layer, peer, col), device_id_type=MESH,
        )

    def start_col(ch, par, value):
        height = value.shape[0]
        col_buf[ch, par, col, 0:height] = value
        for at, peer in enumerate(col_peers):
            col_copy(ch, par, col, at, height, peer).start()

    def finish_col(ch, par, height):
        for at, peer in enumerate(col_peers):
            col_copy(ch, par, peer, at, height, peer).wait_recv()
        total = col_buf[ch, par, 0, 0:height]
        for slot in range(1, COLS):
            total = total + col_buf[ch, par, slot, 0:height]
        return total

    def drain_col(par, height):
        for ch in range(HALVES):
            for at, peer in enumerate(col_peers):
                col_copy(ch, par, col, at, height, peer).wait_send()

    def start_row(ch, par, value):
        height, width = value.shape
        row_buf[ch, par, row, 0:height, 0:width] = value
        for at, peer in enumerate(row_peers):
            row_copy(ch, par, row, at, height, width, peer).start()

    def finish_row(ch, par, height, width):
        for at, peer in enumerate(row_peers):
            row_copy(ch, par, peer, at, height, width, peer).wait_recv()
        total = row_buf[ch, par, 0, 0:height, 0:width]
        for slot in range(1, ROWS):
            total = total + row_buf[ch, par, slot, 0:height, 0:width]
        return total

    def drain_row(par, height, width):
        for ch in range(HALVES):
            for at, peer in enumerate(row_peers):
                row_copy(ch, par, row, at, height, width, peer).wait_send()

    phases = (
        (0, 2, child_wt, child_factor, 2),
        (2, 2 * layer, root_wt, root_factor, PAIRS + 2 * layer),
        (1, 0, child_wt, child_factor, 0),
    )

    def placed(src, dst, recv, send, to_layer, to_row, to_col, wanted, finish):
        here = jnp.logical_and(
            to_layer == layer, jnp.logical_and(to_row == row, to_col == col)
        )

        @pl.when(jnp.logical_and(wanted, jnp.logical_not(here)))
        def _():
            copy = pltpu.make_async_remote_copy(
                src_ref=src, dst_ref=dst, send_sem=send, recv_sem=recv,
                device_id=(to_layer, to_row, to_col), device_id_type=MESH,
            )
            copy.wait_send() if finish else copy.start()

        if not finish:
            @pl.when(jnp.logical_and(wanted, here))
            def _():
                pltpu.make_async_copy(src, dst, recv).start()

    def arrived(ref, sem):
        pltpu.make_async_copy(ref, ref, sem).wait()

    def gather_z(phase, finish=False):
        base, first, wt, factor, _ = phases[phase]
        for which in range(2):
            pair, team = first + which, base + 4 * which
            needed = col2 >= row4
            for kind, (src, dst, wanted) in enumerate((
                (wt.at[2 * pair], a0_buf.at[rowm, col], needed),
                (factor.at[2 * pair + 1, 2 * pair], c_buf.at[row4, col], True),
                (wt.at[2 * pair + 1], a1_buf.at[row4, col], needed),
            )):
                placed(
                    src, dst, z_recv.at[kind], z_send.at[phase, which, kind],
                    layer, row, team, wanted, finish,
                )

    def team_copy(src, dst, send, recv, to_row):
        return pltpu.make_async_remote_copy(
            src_ref=src, dst_ref=dst, send_sem=send, recv_sem=recv,
            device_id=(layer, to_row, col), device_id_type=MESH,
        )

    def tail(ref, slot, part):
        return ref.at[slot, pl.ds(2 * part, COLS - 2 * part)]

    def a0_copy(part, slot, to):
        where = tail(a0_buf, slot, part)
        return team_copy(where, where, xy_send.at[0, to], xy_recv.at[0, slot], 4 * row4 + to)

    def c_copy(part, slot, to):
        where = tail(c_buf, slot, part)
        return team_copy(where, where, xy_send.at[1, to], xy_recv.at[1, slot], 4 * to + rowm)

    def a1_copy(part, slot, to):
        where = tail(a1_buf, slot, part)
        return team_copy(where, where, xy_send.at[2, to], xy_recv.at[2, slot], 4 * to + rowm)

    def part_copy(slot, to):
        return team_copy(
            x_out.at[pl.ds(2 * to, 2)], x_in.at[slot],
            xy_send.at[3, to], xy_recv.at[3, slot], 4 * row4 + to,
        )

    def in_team(phase, work):
        pl.when(lax.rem(col, 4) == phases[phase][0])(work)

    def gather_ac():
        arrived(c_buf.at[row4], z_recv.at[1])
        for to in range(4):
            @pl.when(row4 != to)
            def _():
                c_copy(to, row4, to).start()
        for part in range(4):
            @pl.when(row4 == part)
            def _():
                arrived(tail(a0_buf, rowm, part), z_recv.at[0])
                for to in range(4):
                    @pl.when(rowm != to)
                    def _():
                        a0_copy(part, rowm, to).start()

    def gather_a1():
        for part in range(4):
            @pl.when(row4 == part)
            def _():
                arrived(tail(a1_buf, row4, part), z_recv.at[2])
                for to in range(4):
                    if to != part:
                        a1_copy(part, row4, to).start()

    def first_product():
        for part in range(4):
            @pl.when(row4 == part)
            def _():
                for slot in range(4):
                    @pl.when(rowm != slot)
                    def _():
                        a0_copy(part, slot, slot).wait_recv()
                    if slot != part:
                        c_copy(part, slot, slot).wait_recv()
        t_buf[...] = jnp.zeros_like(t_buf)

        @pl.loop(2 * row4, COLS)
        def _(at):
            t_buf[...] += dot_t(
                a0_buf[:, at].reshape(4 * THIN, WIDE), c_buf[:, at].reshape(4 * THIN, WIDE)
            )

    def second_product():
        for slot in range(4):
            @pl.when(row4 != slot)
            def _():
                a1_copy(slot, slot, slot).wait_recv()
        for at in range(COLS):
            deep = at // 2 + 1
            x_out[at] = dot_n(
                t_buf[:, 0:deep * THIN], a1_buf[0:deep, at].reshape(deep * THIN, WIDE)
            )

    def send_parts():
        for to in range(4):
            @pl.when(rowm != to)
            def _():
                part_copy(rowm, to).start()

    def spread(phase, finish=False):
        if finish:
            for part in range(4):
                @pl.when(row4 == part)
                def _():
                    for to in range(4):
                        @pl.when(rowm != to)
                        def _():
                            a0_copy(part, rowm, to).wait_send()
                        if to != part:
                            a1_copy(part, row4, to).wait_send()
            for to in range(4):
                @pl.when(row4 != to)
                def _():
                    c_copy(to, row4, to).wait_send()
                @pl.when(rowm != to)
                def _():
                    part_copy(rowm, to).wait_send()
        else:
            x_in[rowm] = x_out[pl.ds(2 * rowm, 2)]
            for slot in range(4):
                @pl.when(rowm != slot)
                def _():
                    part_copy(slot, slot).wait_recv()
            for side in range(2):
                x_buf[side] = -(
                    (x_in[0, side] + x_in[1, side]) + (x_in[2, side] + x_in[3, side])
                )
        slot = phases[phase][4] + col // 4
        for to in range(2):
            if phase != 1 and to == 1:
                continue
            for side in range(2):
                for part in range(4):
                    placed(
                        x_buf.at[side, pl.ds(part * THIN, THIN)],
                        superw.at[slot, pl.ds(0, THIN), pl.ds(WIDE, WIDE)],
                        x_recv.at[slot], x_send.at[to, side, part],
                        layer if to == 0 else 1 - layer,
                        4 * row4 + part, 2 * rowm + side, True, finish,
                    )

    def inverse_ready(at):
        arrived(superw.at[at, pl.ds(0, THIN), pl.ds(WIDE, WIDE)], x_recv.at[at])

    def fill_superw():
        for base, wt in ((0, child_wt), (PAIRS, root_wt)):
            for pair in range(PAIRS):
                superw[base + pair, 0:THIN, 0:WIDE] = wt[2 * pair]
                superw[base + pair, THIN:, WIDE:] = wt[2 * pair + 1]
                superw[base + pair, THIN:, 0:WIDE] = jnp.zeros((THIN, WIDE), jnp.float32)

    def child_trailing(value, block, first):
        for later in range(first, PAIRS):
            acc_f[later] += dot_t(value, pair_rows(child_factor, later, block))

    def lifting(value, block):
        for at in range(PAIRS):
            lift_buf[at] += dot_t(value, pair_rows(coupling, at, block))

    fine = half // HALVES
    child_rows = [slice(ch * half, (ch + 1) * half) for ch in range(HALVES)]
    root_rows = [slice(ch * fine, (ch + 1) * fine) for ch in range(HALVES)]

    def child_value(ch, block):
        value = finish_row(ch, block % 2, half, WIDE)
        rows, pair, side = child_rows[ch], block // 2, block % 2
        u_ref[pair, rows, side * WIDE:(side + 1) * WIDE] = value
        if side == 0:
            acc_f[pair, rows, THIN:] += dot_t(value, child_factor[block + 1, block])
        else:
            acc_f[pair + 1, rows] += dot_t(value, pair_rows(child_factor, pair + 1, block))

    def child_block(block):
        return u_ref[block // 2, :, (block % 2) * WIDE:(block % 2 + 1) * WIDE]

    loads[0].wait()
    for ch in range(HALVES):
        start_row(ch, 0, dot_n(child_rhs[0, child_rows[ch], 0:THIN], child_wt[0]))
    for load in loads[1:]:
        load.wait()
    gather_z(0)
    gather_z(1)
    fill_superw()
    for block in range(1, SINGLES):
        par = block % 2
        pair, side = block // 2, block % 2
        low, high = side * THIN, (side + 1) * THIN
        for ch in range(HALVES):
            child_value(ch, block - 1)
            start_col(ch, par, pack(acc_f[pair, child_rows[ch], low:high]))
        for phase in range(2):
            if block == 1:
                in_team(phase, gather_ac)
            if block == 2:
                in_team(phase, gather_a1)
                in_team(phase, first_product)
            if block == 3:
                in_team(phase, lambda: spread(phase))
        drain_row(1 - par, half, WIDE)
        child_trailing(child_block(block - 1), block - 1, pair + 1)
        for ch in range(HALVES):
            total = unpack(finish_col(ch, par, half // 2))
            pending = child_rhs[pair, child_rows[ch], low:high] - total
            start_row(ch, par, dot_n(pending, child_wt[block]))
        for phase in range(2):
            if block == 2:
                in_team(phase, second_product)
                in_team(phase, send_parts)
        drain_col(par, half // 2)
        lifting(child_block(block - 1), block - 1)

    def child_pair(ch, pair):
        value = finish_row(ch, pair % 2, half, 2 * WIDE)
        rows = child_rows[ch]
        u_ref[pair, rows] = value
        if pair + 1 < PAIRS:
            for side in range(2):
                acc_f[pair + 1, rows] += dot_t(
                    value[:, side * WIDE:(side + 1) * WIDE],
                    pair_rows(child_factor, pair + 1, 2 * pair + side),
                )

    for pair in range(SINGLES // 2, PAIRS):
        par = pair % 2
        opening = pair == SINGLES // 2
        for ch in range(HALVES):
            if opening:
                child_value(ch, SINGLES - 1)
            else:
                child_pair(ch, pair - 1)
            start_col(ch, par, acc_f[pair, child_rows[ch]])
        if opening:
            drain_row(1 - par, half, WIDE)
            child_trailing(child_block(SINGLES - 1), SINGLES - 1, pair + 1)
            lifting(child_block(SINGLES - 1), SINGLES - 1)
        else:
            drain_row(1 - par, half, 2 * WIDE)
            for block in (2 * pair - 2, 2 * pair - 1):
                child_trailing(child_block(block), block, pair + 1)
        inverse_ready(pair)
        for ch in range(HALVES):
            pending = child_rhs[pair, child_rows[ch]] - finish_col(ch, par, half)
            start_row(ch, par, dot_n(pending, superw[pair]))
        if not opening:
            for block in (2 * pair - 2, 2 * pair - 1):
                lifting(child_block(block), block)
        drain_col(par, half)
    for ch in range(HALVES):
        child_pair(ch, PAIRS - 1)
    value = u_ref[PAIRS - 1]

    def lift_copy(at):
        return pltpu.make_async_remote_copy(
            src_ref=lift_buf.at[at, pl.ds(theirs, half)], dst_ref=lift_in.at[at],
            send_sem=lift_send.at[at], recv_sem=lift_recv.at[at],
            device_id=other, device_id_type=MESH,
        )

    for at in range(PAIRS):
        for side in range(2):
            lift_buf[at] += dot_t(
                value[:, side * WIDE:(side + 1) * WIDE],
                pair_rows(coupling, at, 2 * PAIRS - 2 + side),
            )
        lift_copy(at).start()

    def lift_ready(at):
        lift_copy(at).wait_recv()
        acc_r[at] = lift_buf[at, pl.ds(mine, half)] + lift_in[at]
        lift_copy(at).wait_send()

    lift_ready(0)

    def root_residual(pair, par):
        inverse_ready(PAIRS + pair)
        for ch in range(HALVES):
            rows = pl.ds(pl.multiple_of(mine + ch * fine, fine), fine)
            pending = root_rhs[pair, rows] - finish_col(ch, par, fine)
            start_row(ch, par, dot_n(pending, superw[PAIRS + pair]))

    for ch in range(HALVES):
        start_col(ch, 0, acc_r[0, root_rows[ch]])
    drain_row(1, half, 2 * WIDE)
    for at in range(1, PAIRS):
        lift_ready(at)
    root_residual(0, 0)
    gather_z(2)
    drain_col(0, fine)

    def root_forward(pair, carry):
        par = lax.rem(pair, 2)
        for ch in range(HALVES):
            value = finish_row(ch, 1 - par, fine, 2 * WIDE)
            v_ref[pair - 1, root_rows[ch]] = value
            for side in range(2):
                acc_r[pair, root_rows[ch]] += dot_t(
                    value[:, side * WIDE:(side + 1) * WIDE],
                    pair_rows(root_factor, pair, 2 * pair - 2 + side),
                )
            start_col(ch, par, acc_r[pair, root_rows[ch]])
        pl.when(pair == 1)(lambda: in_team(2, gather_ac))
        pl.when(pair == 2)(lambda: in_team(2, gather_a1))
        pl.when(pair == 3)(lambda: in_team(2, send_parts))
        drain_row(1 - par, fine, 2 * WIDE)
        before = v_ref[pair - 1]

        @pl.loop(pair + 1, PAIRS)
        def _(later):
            for side in range(2):
                acc_r[later] += dot_t(
                    before[:, side * WIDE:(side + 1) * WIDE],
                    pair_rows(root_factor, later, 2 * pair - 2 + side),
                )

        root_residual(pair, par)
        pl.when(pair == 1)(lambda: in_team(2, first_product))
        pl.when(pair == 2)(lambda: in_team(2, second_product))
        pl.when(pair == 3)(lambda: in_team(2, lambda: spread(2)))
        drain_col(par, fine)
        return carry

    lax.fori_loop(1, PAIRS, root_forward, 0)

    def s_copy(pair):
        return pltpu.make_async_remote_copy(
            src_ref=s_half.at[pair], dst_ref=s_in.at[pair],
            send_sem=s_send.at[pair], recv_sem=s_recv.at[pair],
            device_id=other, device_id_type=MESH,
        )

    def root_solved(pair):
        s_copy(pair).wait_recv()
        root_out[pair, pl.ds(mine, half)] = s_half[pair]
        root_out[pair, pl.ds(theirs, half)] = s_in[pair]
        s_copy(pair).wait_send()

    def lower(value, pair, earlier):
        for side in range(2):
            acc_c[earlier, :, side * WIDE:(side + 1) * WIDE] += dot_n(
                value, pair_rows(coupling, pair, 2 * earlier + side)
            )

    for ch in range(HALVES):
        value = finish_row(ch, 1, fine, 2 * WIDE)
        v_ref[PAIRS - 1, root_rows[ch]] = value
        start_col(ch, 0, dot_t(value, superw[2 * PAIRS - 1]))
    drain_row(1, fine, 2 * WIDE)

    def root_backward(step, carry):
        par = lax.rem(step, 2)
        pair = PAIRS - 1 - step
        after = pair + 1
        for ch in range(HALVES):
            rows = root_rows[ch]
            value = finish_col(ch, 1 - par, fine)
            s_half[after, rows] = value
            for side in range(2):
                acc_b[pair, rows, side * WIDE:(side + 1) * WIDE] += dot_n(
                    value, pair_rows(root_factor, after, 2 * pair + side)
                )
            start_row(ch, 1 - par, acc_b[pair, rows])
        s_copy(after).start()
        drain_col(1 - par, fine)
        solved = s_half[after]

        @pl.loop(0, pair)
        def _(earlier):
            for side in range(2):
                acc_b[earlier, :, side * WIDE:(side + 1) * WIDE] += dot_n(
                    solved, pair_rows(root_factor, after, 2 * earlier + side)
                )

        for ch in range(HALVES):
            pending = v_ref[pair, root_rows[ch]] - finish_row(ch, 1 - par, fine, 2 * WIDE)
            start_col(ch, par, dot_t(pending, superw[PAIRS + pair]))
        drain_row(1 - par, fine, 2 * WIDE)
        root_solved(after)
        both = root_out[after]

        @pl.loop(0, PAIRS)
        def _(earlier):
            lower(both, after, earlier)

        return carry

    lax.fori_loop(1, PAIRS, root_backward, 0)
    for ch in range(HALVES):
        s_half[0, root_rows[ch]] = finish_col(ch, 1, fine)
    s_copy(0).start()
    drain_col(1, fine)
    root_solved(0)

    last = root_out[0]
    lower(last, 0, PAIRS - 1)
    for ch in range(HALVES):
        start_row(ch, 1, acc_c[PAIRS - 1, child_rows[ch]])
    for earlier in range(PAIRS - 1):
        lower(last, 0, earlier)
    for at in range(SINGLES // 2):
        inverse_ready(at)

    def child_residual(pair, par):
        for ch in range(HALVES):
            pending = u_ref[pair, child_rows[ch]] - finish_row(ch, 1 - par, half, 2 * WIDE)
            start_col(ch, par, dot_t(pending, superw[pair]))
        drain_row(1 - par, half, 2 * WIDE)

    child_residual(PAIRS - 1, 0)

    def write_pair(result, source, pair):
        for side in range(2):
            result[:, 2 * pair + side] = source[pair, :, side * THIN:(side + 1) * THIN]

    for pair in range(PAIRS):
        write_pair(root_result, root_out, pair)

    def child_backward(step, carry):
        par = lax.rem(step, 2)
        pair = PAIRS - 1 - step
        after = pair + 1
        for ch in range(HALVES):
            rows = child_rows[ch]
            value = finish_col(ch, 1 - par, half)
            child_out[after, rows] = value
            for side in range(2):
                acc_c[pair, rows, side * WIDE:(side + 1) * WIDE] += dot_n(
                    value, pair_rows(child_factor, after, 2 * pair + side)
                )
            start_row(ch, 1 - par, acc_c[pair, rows])
        drain_col(1 - par, half)
        solved = child_out[after]

        @pl.loop(0, pair)
        def _(earlier):
            for side in range(2):
                acc_c[earlier, :, side * WIDE:(side + 1) * WIDE] += dot_n(
                    solved, pair_rows(child_factor, after, 2 * earlier + side)
                )

        child_residual(pair, par)
        for phase in range(3):
            @pl.when(step == phase + 1)
            def _():
                gather_z(phase, True)
                in_team(phase, lambda: spread(phase, True))

        return carry

    lax.fori_loop(1, PAIRS, child_backward, 0)
    for ch in range(HALVES):
        child_out[0, child_rows[ch]] = finish_col(ch, 1, half)
    for pair in range(PAIRS):
        write_pair(child_result, child_out, pair)
    drain_col(1, half)


def local(root_rhs, child_rhs, root_factor, child_factor, coupling, root_inverse, child_inverse):
    nrhs = root_rhs.shape[0]
    half = nrhs // 2
    vmem = pl.BlockSpec(memory_space=pltpu.VMEM)
    f32 = jnp.float32
    dma = pltpu.SemaphoreType.DMA
    root, child = pl.pallas_call(
        kernel,
        out_shape=(
            jax.ShapeDtypeStruct((nrhs, 2 * PAIRS, THIN), f32),
            jax.ShapeDtypeStruct((nrhs, 2 * PAIRS, THIN), f32),
        ),
        in_specs=[vmem] * 2 + [pl.BlockSpec(memory_space=pltpu.HBM)] * 5,
        out_specs=[vmem] * 2,
        scratch_shapes=[
            pltpu.VMEM((PAIRS, nrhs, 2 * THIN), f32),
            pltpu.VMEM((PAIRS, nrhs, 2 * THIN), f32),
            pltpu.VMEM((PAIRS, nrhs, 2 * THIN), f32),
            pltpu.VMEM((PAIRS, nrhs, 2 * THIN), f32),
            pltpu.VMEM(root_factor.shape, f32),
            pltpu.VMEM(root_factor.shape, f32),
            pltpu.VMEM(root_factor.shape, f32),
            pltpu.VMEM((2 * PAIRS, THIN, WIDE), f32),
            pltpu.VMEM((2 * PAIRS, THIN, WIDE), f32),
            pltpu.VMEM((PAIRS, nrhs, 2 * WIDE), f32),
            pltpu.VMEM((PAIRS, half, 2 * WIDE), f32),
            pltpu.VMEM((PAIRS, half, 2 * THIN), f32),
            pltpu.VMEM((PAIRS, half, 2 * THIN), f32),
            pltpu.VMEM((PAIRS, nrhs, 2 * THIN), f32),
            pltpu.VMEM((PAIRS, half, 2 * THIN), f32),
            pltpu.VMEM((PAIRS, half, 2 * WIDE), f32),
            pltpu.VMEM((PAIRS, nrhs, 2 * WIDE), f32),
            pltpu.VMEM((2 * PAIRS, 2 * THIN, 2 * WIDE), f32),
            pltpu.VMEM((HALVES, 2, COLS, half, 2 * THIN), f32),
            pltpu.VMEM((HALVES, 2, ROWS, half, 2 * WIDE), f32),
            pltpu.VMEM((PAIRS, nrhs, 2 * THIN), f32),
            pltpu.VMEM((PAIRS, half, 2 * THIN), f32),
            pltpu.VMEM((4, COLS, THIN, WIDE), f32),
            pltpu.VMEM((4, COLS, THIN, WIDE), f32),
            pltpu.VMEM((4, COLS, THIN, WIDE), f32),
            pltpu.VMEM((4 * THIN, 4 * THIN), f32),
            pltpu.VMEM((COLS, 4 * THIN, WIDE), f32),
            pltpu.VMEM((4, 2, 4 * THIN, WIDE), f32),
            pltpu.VMEM((2, 4 * THIN, WIDE), f32),
            dma((HALVES, 2, COLS)), dma((HALVES, 2, COLS)),
            dma((HALVES, 2, ROWS)), dma((HALVES, 2, ROWS)),
            dma((PAIRS,)), dma((PAIRS,)), dma((PAIRS,)), dma((PAIRS,)),
            dma((3, 2, 3)), dma((3,)), dma((4, 4)), dma((4, 4)),
            dma((2, 2, 4)), dma((2 * PAIRS,)), dma((5,)),
        ],
        compiler_params=pltpu.CompilerParams(
            collective_id=0, has_side_effects=True, vmem_limit_bytes=60 << 20
        ),
    )(
        root_rhs, child_rhs[0],
        root_factor, child_factor[0], coupling[0],
        jnp.swapaxes(root_inverse, 1, 2), jnp.swapaxes(child_inverse[0], 1, 2),
    )
    return root, child[None]


def solution(mesh):
    in_specs = (
        P(None, None, "row"),
        P("layer", None, None, "row"),
        P(None, None, "row", "col"),
        P("layer", None, None, "row", "col"),
        P("layer", None, None, "row", "col"),
        P(None, "col", "row"),
        P("layer", None, "col", "row"),
    )
    out_specs = (P(None, None, "row"), P("layer", None, None, "row"))
    return jax.shard_map(local, mesh=mesh, in_specs=in_specs, out_specs=out_specs, check_vma=False)
```

```python
import jax
import jax.numpy as jnp
from jax import lax
from jax.experimental import pallas as pl
from jax.experimental.pallas import tpu as pltpu
from jax.sharding import PartitionSpec as P

MESH = pl.DeviceIdType.MESH
PAIRS = 4
ROWS = 16
COLS = 8
THIN = 64
WIDE = 128
SINGLES = 4
HALVES = 2


def halves(x):
    high = x.astype(jnp.bfloat16)
    return high, (x - high.astype(jnp.float32)).astype(jnp.bfloat16)


def product(x, y, dims):
    (x_high, x_low), (y_high, y_low) = halves(x), halves(y)

    def one(left, right):
        return lax.dot_general(left, right, (dims, ((), ())), preferred_element_type=jnp.float32)

    return one(x_high, y_high) + (one(x_high, y_low) + one(x_low, y_high))


def dot_t(x, y):
    return product(x, y, ((1,), (1,)))


def dot_n(x, y):
    return product(x, y, ((1,), (0,)))


def pack(x):
    half = x.shape[0] // 2
    return jnp.concatenate([x[:half], x[half:]], axis=1)


def unpack(x):
    half = x.shape[1] // 2
    return jnp.concatenate([x[:, :half], x[:, half:]], axis=0)


def pair_rows(ref, pair, block):
    return ref[pl.ds(2 * pair, 2), block].reshape(2 * THIN, WIDE)


def kernel(
    root_rhs_in, child_rhs_in, root_factor_hbm, child_factor_hbm, coupling_hbm, root_wt_hbm,
    child_wt_hbm,
    root_result, child_result,
    root_rhs, child_rhs, root_out, child_out,
    root_factor, child_factor, coupling, root_wt, child_wt,
    u_ref, v_ref, s_half, s_in, acc_f, acc_r, acc_b, acc_c, superw,
    col_buf, row_buf, lift_buf, lift_in, a0_buf, c_buf, a1_buf, t_buf, x_out, x_in, x_buf,
    col_send, col_recv, row_send, row_recv, lift_send, lift_recv, s_send, s_recv,
    z_send, z_recv, xy_send, xy_recv, x_send, x_recv, in_sem,
):
    layer = lax.axis_index("layer")
    row = lax.axis_index("row")
    col = lax.axis_index("col")
    other = (1 - layer, row, col)
    col_peers = [lax.rem(col + k, COLS) for k in range(1, COLS)]
    row4, rowm = row // 4, lax.rem(row, 4)
    offsets = sorted(
        ((y, x) for y in range(4) for x in range(4) if y or x),
        key=lambda at: -(min(at[0], 4 - at[0]) + min(at[1], 4 - at[1])),
    )
    row_peers = [4 * lax.rem(row4 + y, 4) + lax.rem(rowm + x, 4) for y, x in offsets]
    col2, colm = col // 2, lax.rem(col, 2)
    nrhs = child_rhs.shape[1]
    half = nrhs // 2
    mine = pl.multiple_of(layer * half, half)
    theirs = pl.multiple_of((1 - layer) * half, half)

    loads = [
        pltpu.make_async_copy(src, dst, in_sem.at[at])
        for at, (src, dst) in enumerate((
            (child_wt_hbm, child_wt), (child_factor_hbm, child_factor),
            (coupling_hbm, coupling), (root_wt_hbm, root_wt), (root_factor_hbm, root_factor),
        ))
    ]
    for load in loads:
        load.start()
    barrier = pltpu.get_barrier_semaphore()
    for peer in col_peers:
        pl.semaphore_signal(barrier, inc=1, device_id=(layer, row, peer), device_id_type=MESH)
    for peer in row_peers:
        pl.semaphore_signal(barrier, inc=1, device_id=(layer, peer, col), device_id_type=MESH)
    pl.semaphore_signal(barrier, inc=1, device_id=other, device_id_type=MESH)
    for block in range(2 * PAIRS):
        at = (block // 2, slice(None), slice((block % 2) * THIN, (block % 2 + 1) * THIN))
        child_rhs[at] = child_rhs_in[:, block]
        root_rhs[at] = root_rhs_in[:, block]
    for ref in (acc_f, acc_b, acc_c, lift_buf):
        ref[...] = jnp.zeros_like(ref)
    pl.semaphore_wait(barrier, COLS + ROWS - 1)

    def col_copy(ch, par, slot, at, height, peer):
        where = col_buf.at[ch, par, slot, pl.ds(0, height)]
        return pltpu.make_async_remote_copy(
            src_ref=where, dst_ref=where,
            send_sem=col_send.at[ch, par, at], recv_sem=col_recv.at[ch, par, slot],
            device_id=(layer, row, peer), device_id_type=MESH,
        )

    def row_copy(ch, par, slot, at, height, width, peer):
        where = row_buf.at[ch, par, slot, pl.ds(0, height), pl.ds(0, width)]
        return pltpu.make_async_remote_copy(
            src_ref=where, dst_ref=where,
            send_sem=row_send.at[ch, par, at], recv_sem=row_recv.at[ch, par, slot],
            device_id=(layer, peer, col), device_id_type=MESH,
        )

    def start_col(ch, par, value):
        height = value.shape[0]
        col_buf[ch, par, col, 0:height] = value
        for at, peer in enumerate(col_peers):
            col_copy(ch, par, col, at, height, peer).start()

    def finish_col(ch, par, height):
        for at, peer in enumerate(col_peers):
            col_copy(ch, par, peer, at, height, peer).wait_recv()
        total = col_buf[ch, par, 0, 0:height]
        for slot in range(1, COLS):
            total = total + col_buf[ch, par, slot, 0:height]
        return total

    def drain_col(par, height):
        for ch in range(HALVES):
            for at, peer in enumerate(col_peers):
                col_copy(ch, par, col, at, height, peer).wait_send()

    def start_row(ch, par, value):
        height, width = value.shape
        row_buf[ch, par, row, 0:height, 0:width] = value
        for at, peer in enumerate(row_peers):
            row_copy(ch, par, row, at, height, width, peer).start()

    def finish_row(ch, par, height, width):
        for at, peer in enumerate(row_peers):
            row_copy(ch, par, peer, at, height, width, peer).wait_recv()
        total = row_buf[ch, par, 0, 0:height, 0:width]
        for slot in range(1, ROWS):
            total = total + row_buf[ch, par, slot, 0:height, 0:width]
        return total

    def drain_row(par, height, width):
        for ch in range(HALVES):
            for at, peer in enumerate(row_peers):
                row_copy(ch, par, row, at, height, width, peer).wait_send()

    phases = (
        (0, 2, child_wt, child_factor, 2),
        (2, 2 * layer, root_wt, root_factor, PAIRS + 2 * layer),
        (1, 0, child_wt, child_factor, 0),
    )

    def placed(src, dst, recv, send, to_layer, to_row, to_col, wanted, finish):
        here = jnp.logical_and(
            to_layer == layer, jnp.logical_and(to_row == row, to_col == col)
        )

        @pl.when(jnp.logical_and(wanted, jnp.logical_not(here)))
        def _():
            copy = pltpu.make_async_remote_copy(
                src_ref=src, dst_ref=dst, send_sem=send, recv_sem=recv,
                device_id=(to_layer, to_row, to_col), device_id_type=MESH,
            )
            copy.wait_send() if finish else copy.start()

        if not finish:
            @pl.when(jnp.logical_and(wanted, here))
            def _():
                pltpu.make_async_copy(src, dst, recv).start()

    def arrived(ref, sem):
        pltpu.make_async_copy(ref, ref, sem).wait()

    def gather_z(phase, finish=False):
        base, first, wt, factor, _ = phases[phase]
        for which in range(2):
            pair, team = first + which, base + 4 * which
            needed = col2 >= row4
            for kind, (src, dst, wanted) in enumerate((
                (wt.at[2 * pair], a0_buf.at[rowm, col], needed),
                (factor.at[2 * pair + 1, 2 * pair], c_buf.at[row4, col], True),
                (wt.at[2 * pair + 1], a1_buf.at[row4, col], needed),
            )):
                placed(
                    src, dst, z_recv.at[kind], z_send.at[phase, which, kind],
                    layer, row, team, wanted, finish,
                )

    def team_copy(src, dst, send, recv, to_row):
        return pltpu.make_async_remote_copy(
            src_ref=src, dst_ref=dst, send_sem=send, recv_sem=recv,
            device_id=(layer, to_row, col), device_id_type=MESH,
        )

    def tail(ref, slot, part):
        return ref.at[slot, pl.ds(2 * part, COLS - 2 * part)]

    def a0_copy(part, slot, to):
        where = tail(a0_buf, slot, part)
        return team_copy(where, where, xy_send.at[0, to], xy_recv.at[0, slot], 4 * row4 + to)

    def c_copy(part, slot, to):
        where = tail(c_buf, slot, part)
        return team_copy(where, where, xy_send.at[1, to], xy_recv.at[1, slot], 4 * to + rowm)

    def a1_copy(part, slot, to):
        where = tail(a1_buf, slot, part)
        return team_copy(where, where, xy_send.at[2, to], xy_recv.at[2, slot], 4 * to + rowm)

    def part_copy(slot, to):
        return team_copy(
            x_out.at[pl.ds(2 * to, 2)], x_in.at[slot],
            xy_send.at[3, to], xy_recv.at[3, slot], 4 * row4 + to,
        )

    def in_team(phase, work):
        pl.when(lax.rem(col, 4) == phases[phase][0])(work)

    def gather_ac():
        arrived(c_buf.at[row4], z_recv.at[1])
        for to in range(4):
            @pl.when(row4 != to)
            def _():
                c_copy(to, row4, to).start()
        for part in range(4):
            @pl.when(row4 == part)
            def _():
                arrived(tail(a0_buf, rowm, part), z_recv.at[0])
                for to in range(4):
                    @pl.when(rowm != to)
                    def _():
                        a0_copy(part, rowm, to).start()

    def gather_a1():
        for part in range(4):
            @pl.when(row4 == part)
            def _():
                arrived(tail(a1_buf, row4, part), z_recv.at[2])
                for to in range(4):
                    if to != part:
                        a1_copy(part, row4, to).start()

    def first_product():
        for part in range(4):
            @pl.when(row4 == part)
            def _():
                for slot in range(4):
                    @pl.when(rowm != slot)
                    def _():
                        a0_copy(part, slot, slot).wait_recv()
                    if slot != part:
                        c_copy(part, slot, slot).wait_recv()
        t_buf[...] = jnp.zeros_like(t_buf)

        @pl.loop(2 * row4, COLS)
        def _(at):
            t_buf[...] += dot_t(
                a0_buf[:, at].reshape(4 * THIN, WIDE), c_buf[:, at].reshape(4 * THIN, WIDE)
            )

    def second_product():
        for slot in range(4):
            @pl.when(row4 != slot)
            def _():
                a1_copy(slot, slot, slot).wait_recv()
        for at in range(COLS):
            deep = at // 2 + 1
            x_out[at] = dot_n(
                t_buf[:, 0:deep * THIN], a1_buf[0:deep, at].reshape(deep * THIN, WIDE)
            )

    def send_parts():
        for to in range(4):
            @pl.when(rowm != to)
            def _():
                part_copy(rowm, to).start()

    def spread(phase, finish=False):
        if finish:
            for part in range(4):
                @pl.when(row4 == part)
                def _():
                    for to in range(4):
                        @pl.when(rowm != to)
                        def _():
                            a0_copy(part, rowm, to).wait_send()
                        if to != part:
                            a1_copy(part, row4, to).wait_send()
            for to in range(4):
                @pl.when(row4 != to)
                def _():
                    c_copy(to, row4, to).wait_send()
                @pl.when(rowm != to)
                def _():
                    part_copy(rowm, to).wait_send()
        else:
            x_in[rowm] = x_out[pl.ds(2 * rowm, 2)]
            for slot in range(4):
                @pl.when(rowm != slot)
                def _():
                    part_copy(slot, slot).wait_recv()
            for side in range(2):
                x_buf[side] = -(
                    (x_in[0, side] + x_in[1, side]) + (x_in[2, side] + x_in[3, side])
                )
        slot = phases[phase][4] + col // 4
        for to in range(2):
            if phase != 1 and to == 1:
                continue
            for side in range(2):
                for part in range(4):
                    placed(
                        x_buf.at[side, pl.ds(part * THIN, THIN)],
                        superw.at[slot, pl.ds(0, THIN), pl.ds(WIDE, WIDE)],
                        x_recv.at[slot], x_send.at[to, side, part],
                        layer if to == 0 else 1 - layer,
                        4 * row4 + part, 2 * rowm + side, True, finish,
                    )

    def inverse_ready(at):
        arrived(superw.at[at, pl.ds(0, THIN), pl.ds(WIDE, WIDE)], x_recv.at[at])

    def fill_superw():
        for base, wt in ((0, child_wt), (PAIRS, root_wt)):
            for pair in range(PAIRS):
                superw[base + pair, 0:THIN, 0:WIDE] = wt[2 * pair]
                superw[base + pair, THIN:, WIDE:] = wt[2 * pair + 1]
                superw[base + pair, THIN:, 0:WIDE] = jnp.zeros((THIN, WIDE), jnp.float32)

    def child_trailing(value, block, first):
        for later in range(first, PAIRS):
            acc_f[later] += dot_t(value, pair_rows(child_factor, later, block))

    def lifting(value, block):
        for at in range(PAIRS):
            lift_buf[at] += dot_t(value, pair_rows(coupling, at, block))

    fine = half // HALVES
    child_rows = [slice(ch * half, (ch + 1) * half) for ch in range(HALVES)]
    root_rows = [slice(ch * fine, (ch + 1) * fine) for ch in range(HALVES)]

    def child_value(ch, block):
        value = finish_row(ch, block % 2, half, WIDE)
        rows, pair, side = child_rows[ch], block // 2, block % 2
        u_ref[pair, rows, side * WIDE:(side + 1) * WIDE] = value
        if side == 0:
            acc_f[pair, rows, THIN:] += dot_t(value, child_factor[block + 1, block])
        else:
            acc_f[pair + 1, rows] += dot_t(value, pair_rows(child_factor, pair + 1, block))

    def child_block(block):
        return u_ref[block // 2, :, (block % 2) * WIDE:(block % 2 + 1) * WIDE]

    loads[0].wait()
    for ch in range(HALVES):
        start_row(ch, 0, dot_n(child_rhs[0, child_rows[ch], 0:THIN], child_wt[0]))
    for load in loads[1:]:
        load.wait()
    gather_z(0)
    gather_z(1)
    fill_superw()
    for block in range(1, SINGLES):
        par = block % 2
        pair, side = block // 2, block % 2
        low, high = side * THIN, (side + 1) * THIN
        for ch in range(HALVES):
            child_value(ch, block - 1)
            start_col(ch, par, pack(acc_f[pair, child_rows[ch], low:high]))
        for phase in range(2):
            if block == 1:
                in_team(phase, gather_ac)
            if block == 2:
                in_team(phase, gather_a1)
                in_team(phase, first_product)
            if block == 3:
                in_team(phase, lambda: spread(phase))
        drain_row(1 - par, half, WIDE)
        child_trailing(child_block(block - 1), block - 1, pair + 1)
        for ch in range(HALVES):
            total = unpack(finish_col(ch, par, half // 2))
            pending = child_rhs[pair, child_rows[ch], low:high] - total
            start_row(ch, par, dot_n(pending, child_wt[block]))
        for phase in range(2):
            if block == 2:
                in_team(phase, second_product)
                in_team(phase, send_parts)
        drain_col(par, half // 2)
        lifting(child_block(block - 1), block - 1)

    def child_pair(ch, pair):
        value = finish_row(ch, pair % 2, half, 2 * WIDE)
        rows = child_rows[ch]
        u_ref[pair, rows] = value
        if pair + 1 < PAIRS:
            for side in range(2):
                acc_f[pair + 1, rows] += dot_t(
                    value[:, side * WIDE:(side + 1) * WIDE],
                    pair_rows(child_factor, pair + 1, 2 * pair + side),
                )

    for pair in range(SINGLES // 2, PAIRS):
        par = pair % 2
        opening = pair == SINGLES // 2
        for ch in range(HALVES):
            if opening:
                child_value(ch, SINGLES - 1)
            else:
                child_pair(ch, pair - 1)
            start_col(ch, par, acc_f[pair, child_rows[ch]])
        if opening:
            drain_row(1 - par, half, WIDE)
            child_trailing(child_block(SINGLES - 1), SINGLES - 1, pair + 1)
            lifting(child_block(SINGLES - 1), SINGLES - 1)
        else:
            drain_row(1 - par, half, 2 * WIDE)
            for block in (2 * pair - 2, 2 * pair - 1):
                child_trailing(child_block(block), block, pair + 1)
        inverse_ready(pair)
        for ch in range(HALVES):
            pending = child_rhs[pair, child_rows[ch]] - finish_col(ch, par, half)
            start_row(ch, par, dot_n(pending, superw[pair]))
        if not opening:
            for block in (2 * pair - 2, 2 * pair - 1):
                lifting(child_block(block), block)
        drain_col(par, half)
    for ch in range(HALVES):
        child_pair(ch, PAIRS - 1)
    value = u_ref[PAIRS - 1]

    def lift_copy(at):
        return pltpu.make_async_remote_copy(
            src_ref=lift_buf.at[at, pl.ds(theirs, half)], dst_ref=lift_in.at[at],
            send_sem=lift_send.at[at], recv_sem=lift_recv.at[at],
            device_id=other, device_id_type=MESH,
        )

    for at in range(PAIRS):
        for side in range(2):
            lift_buf[at] += dot_t(
                value[:, side * WIDE:(side + 1) * WIDE],
                pair_rows(coupling, at, 2 * PAIRS - 2 + side),
            )
        lift_copy(at).start()

    def lift_ready(at):
        lift_copy(at).wait_recv()
        acc_r[at] = lift_buf[at, pl.ds(mine, half)] + lift_in[at]
        lift_copy(at).wait_send()

    lift_ready(0)

    def root_residual(pair, par):
        inverse_ready(PAIRS + pair)
        for ch in range(HALVES):
            rows = pl.ds(pl.multiple_of(mine + ch * fine, fine), fine)
            pending = root_rhs[pair, rows] - finish_col(ch, par, fine)
            start_row(ch, par, dot_n(pending, superw[PAIRS + pair]))

    for ch in range(HALVES):
        start_col(ch, 0, acc_r[0, root_rows[ch]])
    drain_row(1, half, 2 * WIDE)
    for at in range(1, PAIRS):
        lift_ready(at)
    root_residual(0, 0)
    gather_z(2)
    drain_col(0, fine)

    def root_forward(pair, carry):
        par = lax.rem(pair, 2)
        for ch in range(HALVES):
            value = finish_row(ch, 1 - par, fine, 2 * WIDE)
            v_ref[pair - 1, root_rows[ch]] = value
            for side in range(2):
                acc_r[pair, root_rows[ch]] += dot_t(
                    value[:, side * WIDE:(side + 1) * WIDE],
                    pair_rows(root_factor, pair, 2 * pair - 2 + side),
                )
            start_col(ch, par, acc_r[pair, root_rows[ch]])
        pl.when(pair == 1)(lambda: in_team(2, gather_ac))
        pl.when(pair == 2)(lambda: in_team(2, gather_a1))
        pl.when(pair == 3)(lambda: in_team(2, send_parts))
        drain_row(1 - par, fine, 2 * WIDE)
        before = v_ref[pair - 1]

        @pl.loop(pair + 1, PAIRS)
        def _(later):
            for side in range(2):
                acc_r[later] += dot_t(
                    before[:, side * WIDE:(side + 1) * WIDE],
                    pair_rows(root_factor, later, 2 * pair - 2 + side),
                )

        root_residual(pair, par)
        pl.when(pair == 1)(lambda: in_team(2, first_product))
        pl.when(pair == 2)(lambda: in_team(2, second_product))
        pl.when(pair == 3)(lambda: in_team(2, lambda: spread(2)))
        drain_col(par, fine)
        return carry

    lax.fori_loop(1, PAIRS, root_forward, 0)

    def s_copy(pair):
        return pltpu.make_async_remote_copy(
            src_ref=s_half.at[pair], dst_ref=s_in.at[pair],
            send_sem=s_send.at[pair], recv_sem=s_recv.at[pair],
            device_id=other, device_id_type=MESH,
        )

    def root_solved(pair):
        s_copy(pair).wait_recv()
        root_out[pair, pl.ds(mine, half)] = s_half[pair]
        root_out[pair, pl.ds(theirs, half)] = s_in[pair]
        s_copy(pair).wait_send()

    def lower(value, pair, earlier):
        for side in range(2):
            acc_c[earlier, :, side * WIDE:(side + 1) * WIDE] += dot_n(
                value, pair_rows(coupling, pair, 2 * earlier + side)
            )

    for ch in range(HALVES):
        value = finish_row(ch, 1, fine, 2 * WIDE)
        v_ref[PAIRS - 1, root_rows[ch]] = value
        start_col(ch, 0, dot_t(value, superw[2 * PAIRS - 1]))
    drain_row(1, fine, 2 * WIDE)

    def root_backward(step, carry):
        par = lax.rem(step, 2)
        pair = PAIRS - 1 - step
        after = pair + 1
        for ch in range(HALVES):
            rows = root_rows[ch]
            value = finish_col(ch, 1 - par, fine)
            s_half[after, rows] = value
            for side in range(2):
                acc_b[pair, rows, side * WIDE:(side + 1) * WIDE] += dot_n(
                    value, pair_rows(root_factor, after, 2 * pair + side)
                )
            start_row(ch, 1 - par, acc_b[pair, rows])
        s_copy(after).start()
        drain_col(1 - par, fine)
        solved = s_half[after]

        @pl.loop(0, pair)
        def _(earlier):
            for side in range(2):
                acc_b[earlier, :, side * WIDE:(side + 1) * WIDE] += dot_n(
                    solved, pair_rows(root_factor, after, 2 * earlier + side)
                )

        for ch in range(HALVES):
            pending = v_ref[pair, root_rows[ch]] - finish_row(ch, 1 - par, fine, 2 * WIDE)
            start_col(ch, par, dot_t(pending, superw[PAIRS + pair]))
        drain_row(1 - par, fine, 2 * WIDE)
        root_solved(after)
        both = root_out[after]

        @pl.loop(0, PAIRS)
        def _(earlier):
            lower(both, after, earlier)

        return carry

    lax.fori_loop(1, PAIRS, root_backward, 0)
    for ch in range(HALVES):
        s_half[0, root_rows[ch]] = finish_col(ch, 1, fine)
    s_copy(0).start()
    drain_col(1, fine)
    root_solved(0)

    last = root_out[0]
    lower(last, 0, PAIRS - 1)
    for ch in range(HALVES):
        start_row(ch, 1, acc_c[PAIRS - 1, child_rows[ch]])
    for earlier in range(PAIRS - 1):
        lower(last, 0, earlier)
    for at in range(SINGLES // 2):
        inverse_ready(at)

    def child_residual(pair, par):
        for ch in range(HALVES):
            pending = u_ref[pair, child_rows[ch]] - finish_row(ch, 1 - par, half, 2 * WIDE)
            start_col(ch, par, dot_t(pending, superw[pair]))
        drain_row(1 - par, half, 2 * WIDE)

    child_residual(PAIRS - 1, 0)

    def write_pair(result, source, pair):
        for side in range(2):
            result[:, 2 * pair + side] = source[pair, :, side * THIN:(side + 1) * THIN]

    for pair in range(PAIRS):
        write_pair(root_result, root_out, pair)

    def child_backward(step, carry):
        par = lax.rem(step, 2)
        pair = PAIRS - 1 - step
        after = pair + 1
        for ch in range(HALVES):
            rows = child_rows[ch]
            value = finish_col(ch, 1 - par, half)
            child_out[after, rows] = value
            for side in range(2):
                acc_c[pair, rows, side * WIDE:(side + 1) * WIDE] += dot_n(
                    value, pair_rows(child_factor, after, 2 * pair + side)
                )
            start_row(ch, 1 - par, acc_c[pair, rows])
        drain_col(1 - par, half)
        solved = child_out[after]

        @pl.loop(0, pair)
        def _(earlier):
            for side in range(2):
                acc_c[earlier, :, side * WIDE:(side + 1) * WIDE] += dot_n(
                    solved, pair_rows(child_factor, after, 2 * earlier + side)
                )

        child_residual(pair, par)
        for phase in range(3):
            @pl.when(step == phase + 1)
            def _():
                gather_z(phase, True)
                in_team(phase, lambda: spread(phase, True))

        return carry

    lax.fori_loop(1, PAIRS, child_backward, 0)
    for ch in range(HALVES):
        child_out[0, child_rows[ch]] = finish_col(ch, 1, half)
    for pair in range(PAIRS):
        write_pair(child_result, child_out, pair)
    drain_col(1, half)


def local(root_rhs, child_rhs, root_factor, child_factor, coupling, root_inverse, child_inverse):
    nrhs = root_rhs.shape[0]
    half = nrhs // 2
    vmem = pl.BlockSpec(memory_space=pltpu.VMEM)
    f32 = jnp.float32
    dma = pltpu.SemaphoreType.DMA
    root, child = pl.pallas_call(
        kernel,
        out_shape=(
            jax.ShapeDtypeStruct((nrhs, 2 * PAIRS, THIN), f32),
            jax.ShapeDtypeStruct((nrhs, 2 * PAIRS, THIN), f32),
        ),
        in_specs=[vmem] * 2 + [pl.BlockSpec(memory_space=pltpu.HBM)] * 5,
        out_specs=[vmem] * 2,
        scratch_shapes=[
            pltpu.VMEM((PAIRS, nrhs, 2 * THIN), f32),
            pltpu.VMEM((PAIRS, nrhs, 2 * THIN), f32),
            pltpu.VMEM((PAIRS, nrhs, 2 * THIN), f32),
            pltpu.VMEM((PAIRS, nrhs, 2 * THIN), f32),
            pltpu.VMEM(root_factor.shape, f32),
            pltpu.VMEM(root_factor.shape, f32),
            pltpu.VMEM(root_factor.shape, f32),
            pltpu.VMEM((2 * PAIRS, THIN, WIDE), f32),
            pltpu.VMEM((2 * PAIRS, THIN, WIDE), f32),
            pltpu.VMEM((PAIRS, nrhs, 2 * WIDE), f32),
            pltpu.VMEM((PAIRS, half, 2 * WIDE), f32),
            pltpu.VMEM((PAIRS, half, 2 * THIN), f32),
            pltpu.VMEM((PAIRS, half, 2 * THIN), f32),
            pltpu.VMEM((PAIRS, nrhs, 2 * THIN), f32),
            pltpu.VMEM((PAIRS, half, 2 * THIN), f32),
            pltpu.VMEM((PAIRS, half, 2 * WIDE), f32),
            pltpu.VMEM((PAIRS, nrhs, 2 * WIDE), f32),
            pltpu.VMEM((2 * PAIRS, 2 * THIN, 2 * WIDE), f32),
            pltpu.VMEM((HALVES, 2, COLS, half, 2 * THIN), f32),
            pltpu.VMEM((HALVES, 2, ROWS, half, 2 * WIDE), f32),
            pltpu.VMEM((PAIRS, nrhs, 2 * THIN), f32),
            pltpu.VMEM((PAIRS, half, 2 * THIN), f32),
            pltpu.VMEM((4, COLS, THIN, WIDE), f32),
            pltpu.VMEM((4, COLS, THIN, WIDE), f32),
            pltpu.VMEM((4, COLS, THIN, WIDE), f32),
            pltpu.VMEM((4 * THIN, 4 * THIN), f32),
            pltpu.VMEM((COLS, 4 * THIN, WIDE), f32),
            pltpu.VMEM((4, 2, 4 * THIN, WIDE), f32),
            pltpu.VMEM((2, 4 * THIN, WIDE), f32),
            dma((HALVES, 2, COLS)), dma((HALVES, 2, COLS)),
            dma((HALVES, 2, ROWS)), dma((HALVES, 2, ROWS)),
            dma((PAIRS,)), dma((PAIRS,)), dma((PAIRS,)), dma((PAIRS,)),
            dma((3, 2, 3)), dma((3,)), dma((4, 4)), dma((4, 4)),
            dma((2, 2, 4)), dma((2 * PAIRS,)), dma((5,)),
        ],
        compiler_params=pltpu.CompilerParams(
            collective_id=0, has_side_effects=True, vmem_limit_bytes=60 << 20
        ),
    )(
        root_rhs, child_rhs[0],
        root_factor, child_factor[0], coupling[0],
        jnp.swapaxes(root_inverse, 1, 2), jnp.swapaxes(child_inverse[0], 1, 2),
    )
    return root, child[None]


def solution(mesh):
    in_specs = (
        P(None, None, "row"),
        P("layer", None, None, "row"),
        P(None, None, "row", "col"),
        P("layer", None, None, "row", "col"),
        P("layer", None, None, "row", "col"),
        P(None, "col", "row"),
        P("layer", None, "col", "row"),
    )
    out_specs = (P(None, None, "row"), P("layer", None, None, "row"))
    return jax.shard_map(local, mesh=mesh, in_specs=in_specs, out_specs=out_specs, check_vma=False)
```
